32 devices in a mesh: dp: 8 (over z, x), ctx: 4 (over y, core).
Axes of the slice: x: 2, y: 2, z: 4, core: 2. Of those that a mesh axis runs over, the one named last changes fastest.
Arguments:
- states: bfloat16 [32, 1024, 960], P('dp', 'ctx'), may hold values from -6 to 6
- teacher: bfloat16 [32, 1024, 960], P('dp', 'ctx'), may hold values from -6 to 6
- validity: int32 [32, 1024], P('dp', 'ctx'), may hold values from 0 to 1, as said below
- chosen: int32 [32, 1024], P('dp', 'ctx'), may hold values from 0 to 1, as said below
- attn_pack: bfloat16 [960, 2560], P(None, ('dp', 'ctx')), may hold values from -1 to 1
- gate_up: bfloat16 [960, 5120], P(None, ('dp', 'ctx')), may hold values from -0.1875 to 0.1875
- down_proj: bfloat16 [960, 2560], P(None, ('dp', 'ctx')), may hold values from -0.125 to 0.125
- norm_gains: float32 [2, 960], replicated, may hold values from 0.25 to 1.75
- router: float32 [960], replicated, may hold values from -0.12 to 0.12
Outputs:
- states_out: bfloat16 [32, 1024, 960], P('dp', 'ctx')
- mse_loss: float32 [], replicated
- states_grad: float32 [32, 1024, 960], P('dp', 'ctx')
- attn_pack_grad: float32 [960, 2560], P(None, ('dp', 'ctx'))
- gate_up_grad: float32 [960, 5120], P(None, ('dp', 'ctx'))
- down_proj_grad: float32 [960, 2560], P(None, ('dp', 'ctx'))
- norm_gains_grad: float32 [2, 960], replicated
- router_grad: float32 [960], replicated
The draws below stay inside these ranges and needn't reach their ends.
Inputs may be any that keep to these rules, and one draw needn't show every extreme that they name: `validity`: the first token of every sequence is valid. `chosen`: each sequence has 640 or 641 selected tokens, the first token always among them.
All inputs are finite; a program needn't handle non-finite values.
Results may differ from the reference program's by a relative error of at most 0.012.
Values may be sent and summed in bfloat16 or wider, within the bound.
No kernel may reach another device: no remote copies, remote signals or barrier semaphores. Data moves between devices by JAX's collectives and lax.ppermute only.
A program may use at most 320 MiB of HBM per device.

```python
import jax
import jax.numpy as jnp
from jax import lax

D = 960
HEADS = 15
KV_HEADS = 5
HEAD = 64
FF = 2560
BLOCK = 256
SEQS = 32
SEQLEN = 1024
CHOSEN = 640


def draw_validity(key, part):
    seq_ids = jnp.arange(SEQS)[:, None]
    thresholds = 300 + 600 * seq_ids // max(SEQS - 1, 1)
    raw_draw = jax.random.randint(key, (SEQS, SEQLEN), 0, 1000)
    places = jnp.arange(SEQLEN)[None, :]
    return jnp.where((raw_draw < thresholds) | (places == 0), 1, 0).astype(jnp.int32)


def draw_chosen(key, part):
    seq_keys = jax.random.split(key, SEQS)
    orders = jax.vmap(lambda seq_key: jax.random.permutation(seq_key, SEQLEN))(seq_keys)
    places = jnp.arange(SEQLEN)[None, :]
    return jnp.where((orders < CHOSEN) | (places == 0), 1, 0).astype(jnp.int32)


def draw_attn_pack(key, part):
    columns = 2 * D + 2 * KV_HEADS * HEAD
    base_draw = jnp.clip(jax.random.normal(key, (D, columns), jnp.float32), -6.0, 6.0)
    column_ids = jnp.arange(columns)[None, :]
    scales = jnp.where(column_ids < D + 2 * KV_HEADS * HEAD, D ** (-0.5), 6.0 * D ** (-0.5))
    return jnp.clip(base_draw * scales, -1.0, 1.0).astype(jnp.bfloat16)


def levels(key, dims, cuts, least, high):
    loudness = 1.0
    for dim, blocks in cuts:
        heights = jax.random.uniform(jax.random.fold_in(jax.random.fold_in(key, 6), dim), (blocks,), jnp.float32, least / len(cuts), high / len(cuts))
        loudness = loudness * jnp.repeat(jnp.exp(heights), dims[dim] // blocks).reshape((-1,) + (1,) * (len(dims) - 1 - dim))
    return loudness


def centred(own_key, shape, deviation, reach, shards=(), kind=jnp.bfloat16):
    drawn = deviation * jax.random.normal(own_key, shape, jnp.float32)
    if shards:
        drawn = drawn * levels(own_key, shape, shards, -0.22, 0.18)
    return jnp.clip(drawn, -reach, reach).astype(kind)


def setup_inputs(seed: int = 0) -> dict:
    key_of = jax.random.split(jax.random.key(seed), 10)
    return {
        "states": centred(key_of[0], (SEQS, SEQLEN, D), 1.0, 6.0, ((0, 8), (1, 4))),
        "teacher": centred(key_of[1], (SEQS, SEQLEN, D), 1.0, 6.0, ((0, 8), (1, 4))),
        "validity": draw_validity(jax.random.fold_in(key_of[9], 71), 0),
        "chosen": draw_chosen(jax.random.fold_in(key_of[9], 71), 0),
        "attn_pack": draw_attn_pack(jax.random.fold_in(key_of[9], 71), 0),
        "gate_up": centred(key_of[5], (D, 2 * FF), D ** -0.5, 0.1875, ((1, 32),)),
        "down_proj": centred(key_of[6], (D, FF), FF ** -0.5, 0.125, ((1, 32),)),
        "norm_gains": jnp.clip(1.0 + 0.15 * jax.random.normal(key_of[7], (2, D), jnp.float32), 0.25, 1.75),
        "router": centred(key_of[8], (D,), 0.02, 0.12, (), jnp.float32),
    }


EPS = 1e-05
THETA = 10000.0
HIGH = lax.Precision.HIGHEST

@jax.custom_vjp
def low(v):
    return lax.optimization_barrier(v.astype(jnp.bfloat16)).astype(jnp.float32)

@jax.custom_vjp
def low_back(v):
    return v

def low_keep(v):
    return (low(v), None)

def low_pass(kept, grad):
    return (grad,)

def back_keep(v):
    return (v, None)

def back_low(kept, grad):
    return (low(grad),)
low.defvjp(low_keep, low_pass)
low_back.defvjp(back_keep, back_low)

def rope_tables(positions):
    half_head = HEAD // 2
    freqs = THETA ** (-(jnp.arange(half_head).astype(jnp.float32) * 2.0 / HEAD))
    angles = positions.astype(jnp.float32)[:, None] * freqs[None, :]
    return (jnp.cos(angles)[:, None, :], jnp.sin(angles)[:, None, :])

def rotate(values, cosine, sine):
    half_head = HEAD // 2
    first = values[..., :half_head]
    second = values[..., half_head:]
    return jnp.concatenate([first * cosine - second * sine, second * cosine + first * sine], axis=-1)

def rms_norm(values, gain_row):
    return values * lax.rsqrt(lax.optimization_barrier(jnp.mean(values * values, axis=-1, keepdims=True)) + EPS) * gain_row

def attend_one(queries, keys, values_in, key_ok):
    scores = low_back(jnp.einsum('qgrh,kgh->grqk', queries, keys, precision=HIGH) * 0.125)
    blocks = jnp.arange(SEQLEN) // BLOCK
    allowed = (blocks[None, :] <= blocks[:, None]) & key_ok[None, :]
    scores = jnp.where(allowed, scores, -jnp.inf)
    probs = jax.nn.softmax(scores, axis=-1)
    return jnp.einsum('grqk,kgh->qgrh', low(probs), values_in, precision=HIGH)
attend_saved = jax.checkpoint(attend_one)

def block_forward(x_group, attn_w, gate_w, down_w, gains, gate_vec, extras):
    valid_f, chosen_f, key_ok, teacher_f, cosine, sine = extras
    count_seq = x_group.shape[0]
    qkv_cols = D + 2 * KV_HEADS * HEAD
    kv_width = KV_HEADS * HEAD
    per_kv = HEADS // KV_HEADS
    normed = low(rms_norm(x_group, gains[0]))
    mixed = jnp.dot(normed, attn_w[:, :qkv_cols], precision=HIGH)
    queries = mixed[..., :D].reshape(count_seq, SEQLEN, HEADS, HEAD)
    keys = mixed[..., D:D + kv_width].reshape(count_seq, SEQLEN, KV_HEADS, HEAD)
    values_in = mixed[..., D + kv_width:].reshape(count_seq, SEQLEN, KV_HEADS, HEAD)
    queries = low(rotate(low_back(queries), cosine, sine)).reshape(count_seq, SEQLEN, KV_HEADS, per_kv, HEAD)
    keys = low(rotate(low_back(keys), cosine, sine))
    values_in = low(low_back(values_in))
    heads_out = lax.map(lambda group_item: attend_saved(*group_item), (queries, keys, values_in, key_ok))
    heads_out = low_back(low(heads_out.reshape(count_seq, SEQLEN, D)))
    attn_out = low_back(jnp.dot(heads_out, attn_w[:, qkv_cols:].T, precision=HIGH))
    inner = x_group + attn_out
    normed_two = low(rms_norm(inner, gains[1]))
    gate_both = jnp.dot(normed_two, gate_w, precision=HIGH)
    gate_part = low_back(gate_both[..., :FF])
    up_part = low_back(gate_both[..., FF:])
    hidden = low(jax.nn.silu(gate_part) * up_part)
    ffn_out = low_back(jnp.dot(hidden, down_w.T, precision=HIGH))
    gate_prob = jax.nn.sigmoid(jnp.dot(x_group, gate_vec, precision=HIGH))
    result = x_group + (chosen_f * gate_prob)[..., None] * (attn_out + ffn_out)
    diff = valid_f[..., None] * (result - teacher_f)
    return (0.5 * jnp.sum(diff * diff), result)

def reference(states, teacher, validity, chosen, attn_pack, gate_up, down_proj, norm_gains, router):
    group_size = 2
    groups = SEQS // group_size
    x_groups = states.astype(jnp.float32).reshape(groups, group_size, SEQLEN, D)
    teacher_groups = teacher.astype(jnp.float32).reshape(groups, group_size, SEQLEN, D)
    valid_groups = validity.reshape(groups, group_size, SEQLEN)
    chosen_groups = chosen.reshape(groups, group_size, SEQLEN)
    weights = (attn_pack.astype(jnp.float32), gate_up.astype(jnp.float32), down_proj.astype(jnp.float32), norm_gains, router)
    cosine, sine = rope_tables(jnp.arange(SEQLEN))

    def group_step(running_sums, group_item):
        x_group, teacher_group, valid_group, chosen_group = group_item
        extras = (valid_group.astype(jnp.float32), chosen_group.astype(jnp.float32), valid_group * chosen_group > 0, teacher_group, cosine, sine)

        def energy_of(x_in, attn_w, gate_w, down_w, gains, gate_vec):
            return block_forward(x_in, attn_w, gate_w, down_w, gains, gate_vec, extras)
        energy, pull, result = jax.vjp(energy_of, x_group, *weights, has_aux=True)
        gradients = pull(jnp.ones_like(energy))
        updated = (running_sums[0] + energy,) + tuple((running + gradient for running, gradient in zip(running_sums[1:], gradients[1:])))
        return (updated, (result.astype(jnp.bfloat16), gradients[0]))
    initial = (jnp.zeros((), jnp.float32),) + tuple((jnp.zeros_like(weight) for weight in weights))
    final_sums, (outputs, input_grads) = lax.scan(group_step, initial, (x_groups, teacher_groups, valid_groups, chosen_groups))
    count = jnp.sum(validity).astype(jnp.float32)
    mse_loss = 2.0 * final_sums[0] / (count * D)
    return (outputs.reshape(SEQS, SEQLEN, D), mse_loss, input_grads.reshape(SEQS, SEQLEN, D), final_sums[1], final_sums[2], final_sums[3], final_sums[4], final_sums[5])
```

```python
import functools

import jax
import jax.numpy as jnp
from jax import lax
from jax.experimental import pallas as pl
from jax.experimental.pallas import tpu as pltpu
from jax.sharding import PartitionSpec as P

D = 960
HEADS = 15
KV_HEADS = 5
HEAD = 64
FF = 2560
CHOSEN = 640
PER_KV = HEADS // KV_HEADS
KV_WIDTH = KV_HEADS * HEAD
QKV_COLS = D + 2 * KV_WIDTH
ROWS = 656
TILE = 256
WIDE = 768
SLAB = 1280
CHUNK = 640
TILES = ((0, 256, 512), (256, 512, 768), (512, ROWS, 768))
NEG = -1e30
VMEM_LIMIT = 62 * 1024 * 1024

EPS = 1e-05
THETA = 10000.0
F32 = jnp.float32
BF16 = jnp.bfloat16


def device_bits():
    found = []
    for name in ("dp", "ctx"):
        count = lax.axis_size(name)
        found += [(name, bit) for bit in reversed(range(count.bit_length() - 1))]
    return found


def swap(value, place):
    name, bit = place
    pairs = [(i, i ^ (1 << bit)) for i in range(lax.axis_size(name))]
    return lax.ppermute(value, name, pairs)


def own_bit(place):
    name, bit = place
    return (lax.axis_index(name) >> bit) & 1


def merge(whole, other, place, ahead):
    low_side = own_bit(place) == 0
    size = whole.shape[0]
    whole, other = [v.reshape(ahead, size // ahead, D) for v in (whole, other)]
    both = [jnp.where(low_side, whole, other), jnp.where(low_side, other, whole)]
    return jnp.stack(both, axis=1).reshape(2 * size, D)


def gather_halves(shard, bits):
    other = swap(shard, bits[0])
    low_side = own_bit(bits[0]) == 0
    halves = [jnp.where(low_side, shard, other), jnp.where(low_side, other, shard)]
    last = len(bits) - 1
    for step in range(1, last + 1):
        moved = []
        for half, spots in zip(halves, routes(bits)):
            spot = spots[step - 1]
            ahead = 1 << sum(1 for s in spots[: step - 1] if s < spot)
            moved.append((half, swap(half, bits[spot]), bits[spot], ahead))
        halves = [merge(*m) for m in moved]
    return halves


def routes(bits):
    count = len(bits)
    far = list(range(1, count - 3))
    return [far + [count - 3, count - 2, count - 1], far + [count - 2, count - 3, count - 1]]


class Scatter:
    def __init__(self, grads, bits):
        self.bits = bits
        self.rows = [g.shape[0] >> (len(bits) - 1) for g in grads]
        self.routes = [r[::-1] for r in routes(bits)]
        self.parts = [[g] for g in grads]
        self.held = [sorted(r) for r in self.routes]
        self.step = 0
        self.part = None
        self.got = []

    def cut(self, parts, held, spot, side, rows):
        ahead = 1 << held.index(spot)
        behind = (1 << (len(held) - held.index(spot) - 1)) * rows
        total = 0.0
        for part in parts:
            cube = part.reshape(ahead, 2, behind, D)
            total = total + lax.dynamic_index_in_dim(cube, side, 1, keepdims=False).astype(F32)
        return total.astype(BF16).reshape(ahead * behind, D)

    def send(self):
        arrive = []
        if self.step < len(self.bits) - 1:
            for i in range(2):
                spot = self.routes[i][self.step]
                mine = own_bit(self.bits[spot])
                parts, held, rows = self.parts[i], self.held[i], self.rows[i]
                out = self.cut(parts, held, spot, 1 - mine, rows)
                self.parts[i] = [self.cut(parts, held, spot, mine, rows)]
                self.held[i] = [h for h in held if h != spot]
                arrive.append(swap(out, self.bits[spot]))
        else:
            low_side = own_bit(self.bits[0]) == 0
            sums = []
            for parts in self.parts:
                sums.append(sum(p.astype(F32) for p in parts))
            out = jnp.where(low_side, sums[1], sums[0]).astype(BF16)
            self.keep = jnp.where(low_side, sums[0], sums[1])
            arrive.append(swap(out, self.bits[0]))
        self.step += 1
        return arrive

    def take(self, arrive):
        if self.step == len(self.bits):
            return self.keep + arrive[0].astype(F32)
        for parts, got in zip(self.parts, arrive):
            parts.append(got)


def advance(scatters, value):
    active = [s for s in scatters if s.part is None]
    if value is not None:
        flat = join(value, *[g for s in active for g in s.got])
        value, flat = flat[0], list(flat[1:])
        for s in active:
            s.got, flat = flat[: len(s.got)], flat[len(s.got) :]
    for s in active:
        s.part = s.take(s.got)
        if s.part is None:
            s.got = s.send()
    return value


def join(*values):
    return lax.optimization_barrier(values)


def all_sum(value, bits):
    for place in bits:
        value = value + swap(value, place)
    return value


def dot(left, right, contract):
    return lax.dot_general(left, right, (contract, ((), ())), preferred_element_type=F32)


def to_sequence(blocks):
    return lax.all_to_all(blocks, "ctx", split_axis=0, concat_axis=0, tiled=True)


def nt(left, right):
    return lax.dot_general(left, right, (((1,), (1,)), ((), ())), preferred_element_type=F32)


def nn(left, right):
    return lax.dot_general(left, right, (((1,), (0,)), ((), ())), preferred_element_type=F32)


def tn(left, right):
    return lax.dot_general(left, right, (((0,), (0,)), ((), ())), preferred_element_type=F32)


def turned(values, cosine, sine):
    half = HEAD // 2
    pieces = []
    for start in range(0, values.shape[1], HEAD):
        head = values[:, start : start + HEAD]
        swapped = jnp.concatenate([head[:, half:], head[:, :half]], axis=1)
        pieces.append(head * cosine + swapped * sine)
    return pieces


def weight_specs(first):
    return [
        pl.BlockSpec((D // KV_HEADS, D), lambda g: (first + g, 0)),
        pl.BlockSpec((HEAD, D), lambda g: (HEADS + first + g, 0)),
        pl.BlockSpec((HEAD, D), lambda g: (first + g, 0)),
    ] + [
        pl.BlockSpec((HEAD, D), lambda g, r=r: (KV_HEADS + PER_KV * (first + g) + r, 0))
        for r in range(PER_KV)
    ]


def attend_kernel(
    x_ref, gain_ref, cos_ref, sin_ref, aux_ref, row_ref, wq_ref, wk_ref, wv_ref, wo0_ref, wo1_ref, wo2_ref,
    n1_ref, q_ref, k_ref, v_ref, o_ref, l_ref, h1_ref,
    bias, keys, vals, lse,
):
    group = pl.program_id(0)

    @pl.when(group == 0)
    def _():
        x = x_ref[...].astype(F32)
        inv = lax.rsqrt(jnp.mean(x * x, axis=-1, keepdims=True) + EPS)
        n1_ref[...] = (x * inv * gain_ref[...]).astype(BF16)
        h1_ref[...] = x
        bias[...] = jnp.where(row_ref[1:2, :] <= aux_ref[:, 2:3], 0.0, NEG)
        keys[...] = jnp.zeros_like(keys)
        vals[...] = jnp.zeros_like(vals)
        lse[...] = jnp.zeros_like(lse)

    packed = jnp.concatenate([wq_ref[...], wk_ref[...], wv_ref[...]], axis=0)
    mixed = nt(n1_ref[...], packed)
    rotated = turned(mixed[:, : D // KV_HEADS + HEAD], cos_ref[...], sin_ref[...])
    key = rotated[PER_KV].astype(BF16)
    value = mixed[:, D // KV_HEADS + HEAD :].astype(BF16)
    k_ref[0] = key
    v_ref[0] = value
    keys[:ROWS] = key
    vals[:ROWS] = value
    for head in range(PER_KV):
        q_ref[head] = rotated[head].astype(BF16)
    lanes = lax.broadcasted_iota(jnp.int32, (1, 128), 1)
    for start, stop, reach in TILES:
        outs = []
        logs = jnp.zeros((stop - start, 128), F32)
        for head in range(PER_KV):
            scores = nt(q_ref[head, start:stop], keys[:reach]) * 0.125 + bias[start:stop, :reach]
            top = jnp.max(scores, axis=-1, keepdims=True)
            expd = jnp.exp(scores - top)
            total = jnp.sum(expd, axis=-1, keepdims=True)
            outs.append(nn(expd.astype(BF16), vals[:reach]) / total)
            logs = jnp.where(lanes == head, top + jnp.log(total), logs)
        o_ref[0, start:stop] = jnp.concatenate(outs, axis=1).astype(BF16)
        lse[start:stop] = logs
    l_ref[0] = lse[...].T[:8]
    h1_ref[...] += nn(o_ref[0], jnp.concatenate([wo0_ref[...], wo1_ref[...], wo2_ref[...]], axis=0))


def attend(x, gain, cosine, sine, aux, row, w_low, w_high):
    whole = lambda *shape: pl.BlockSpec(shape, lambda g: (0,) * len(shape))
    fixed = lambda *shape: pl.BlockSpec(
        shape, lambda g: (0,) * len(shape), pipeline_mode=pl.Buffered(1)
    )
    per = D // KV_HEADS
    return pl.pallas_call(
        attend_kernel,
        grid=(KV_HEADS,),
        in_specs=[
            fixed(ROWS, D),
            fixed(1, D),
            fixed(ROWS, HEAD),
            fixed(ROWS, HEAD),
            fixed(ROWS, 8),
            fixed(8, WIDE),
            *weight_specs(0),
        ],
        out_specs=[
            whole(ROWS, D),
            pl.BlockSpec((PER_KV, ROWS, HEAD), lambda g: (g, 0, 0)),
            pl.BlockSpec((1, ROWS, HEAD), lambda g: (g, 0, 0)),
            pl.BlockSpec((1, ROWS, HEAD), lambda g: (g, 0, 0)),
            pl.BlockSpec((1, ROWS, per), lambda g: (g, 0, 0)),
            pl.BlockSpec((1, 8, WIDE), lambda g: (g, 0, 0)),
            whole(ROWS, D),
        ],
        out_shape=[
            jax.ShapeDtypeStruct((ROWS, D), BF16),
            jax.ShapeDtypeStruct((HEADS, ROWS, HEAD), BF16),
            jax.ShapeDtypeStruct((KV_HEADS, ROWS, HEAD), BF16),
            jax.ShapeDtypeStruct((KV_HEADS, ROWS, HEAD), BF16),
            jax.ShapeDtypeStruct((KV_HEADS, ROWS, per), BF16),
            jax.ShapeDtypeStruct((KV_HEADS, 8, WIDE), F32),
            jax.ShapeDtypeStruct((ROWS, D), F32),
        ],
        scratch_shapes=[
            pltpu.VMEM((ROWS, WIDE), F32),
            pltpu.VMEM((WIDE, HEAD), BF16),
            pltpu.VMEM((WIDE, HEAD), BF16),
            pltpu.VMEM((WIDE, 128), F32),
        ],
        compiler_params=pltpu.CompilerParams(vmem_limit_bytes=VMEM_LIMIT),
        name="attend",
    )(x, gain, cosine, sine, aux, row, w_low, w_low, w_high, w_high, w_high, w_high)


def feed_specs(packs):
    if packs[0].ndim == 2:
        return [
            pl.BlockSpec((SLAB, D), lambda j: (j, 0)),
            pl.BlockSpec((SLAB, D), lambda j: (FF // SLAB + j, 0)),
            pl.BlockSpec((SLAB, D), lambda j: (j, 0)),
        ]
    count, rows, _ = packs[0].shape
    thin = rows // 3
    return [
        pl.BlockSpec((SLAB // (2 * thin), 2 * thin, D), lambda j: (j, 0, 0)),
        pl.BlockSpec((SLAB // (2 * thin), 2 * thin, D), lambda j: (FF // SLAB + j, 0, 0)),
        pl.BlockSpec((SLAB // thin, thin, D), lambda j: (j, 2, 0)),
    ]


def rows_of(ref, start=0, size=SLAB):
    if len(ref.shape) == 2:
        return ref[start : start + size]
    each = ref.shape[1]
    return ref[start // each : (start + size) // each].reshape(size, D)


def feed_kernel(
    h1_ref, x_ref, t_ref, aux_ref, gain_ref, router_ref, wg_ref, wu_ref, wd_ref,
    n2_ref, g_ref, u_ref, hid_ref, y_ref, diff_ref, cols_ref, sums_ref, d_ffn_ref,
):
    step = pl.program_id(0)

    @pl.when(step == 0)
    def _():
        h1 = h1_ref[...]
        inv = lax.rsqrt(jnp.mean(h1 * h1, axis=-1, keepdims=True) + EPS)
        n2_ref[...] = (h1 * inv * gain_ref[...]).astype(BF16)
        diff_ref[...] = h1 - x_ref[...].astype(F32)

    for start in range(0, SLAB, CHUNK):
        span = slice(start, start + CHUNK)
        gate = nt(n2_ref[...], rows_of(wg_ref, start, CHUNK))
        up = nt(n2_ref[...], rows_of(wu_ref, start, CHUNK))
        g_ref[:, span] = gate.astype(BF16)
        u_ref[:, span] = up.astype(BF16)
        hid_ref[:, span] = (gate * jax.nn.sigmoid(gate) * up).astype(BF16)
    diff_ref[...] += nn(hid_ref[...], rows_of(wd_ref))

    @pl.when(step == pl.num_programs(0) - 1)
    def _():
        x = x_ref[...].astype(F32)
        branch = diff_ref[...]
        valid, live = aux_ref[:, 0:1], aux_ref[:, 1:2]
        prob = jax.nn.sigmoid(jnp.sum(x * router_ref[...], axis=-1, keepdims=True))
        mix = live * prob
        result = x + mix * branch
        y_ref[...] = result.astype(BF16)
        diff = valid * (result - t_ref[...].astype(F32))
        d_logit = live * jnp.sum(diff * branch, axis=-1, keepdims=True) * prob * (1.0 - prob)
        diff_ref[...] = diff
        d_ffn_ref[...] = (mix * diff).astype(BF16)
        lanes = lax.broadcasted_iota(jnp.int32, (1, 128), 1)
        cols_ref[...] = jnp.where(lanes == 0, mix, jnp.where(lanes == 1, d_logit, 0.0))
        sums_ref[...] = jnp.concatenate(
            [
                jnp.sum(d_logit * x, axis=0, keepdims=True),
                0.5 * jnp.sum(diff * diff, axis=0, keepdims=True),
                jnp.zeros((6, D), F32),
            ],
            axis=0,
        )


def feed(h1, x, t, aux, gain, router, packs):
    whole = lambda *shape: pl.BlockSpec(shape, lambda j: (0,) * len(shape))
    fixed = lambda *shape: pl.BlockSpec(
        shape, lambda j: (0,) * len(shape), pipeline_mode=pl.Buffered(1)
    )
    return pl.pallas_call(
        feed_kernel,
        grid=(FF // SLAB,),
        in_specs=[
            fixed(ROWS, D),
            fixed(ROWS, D),
            fixed(ROWS, D),
            fixed(ROWS, 8),
            fixed(1, D),
            fixed(1, D),
            *feed_specs(packs),
        ],
        out_specs=[
            whole(ROWS, D),
            pl.BlockSpec((ROWS, SLAB), lambda j: (0, j)),
            pl.BlockSpec((ROWS, SLAB), lambda j: (0, j)),
            pl.BlockSpec((ROWS, SLAB), lambda j: (0, j)),
            whole(ROWS, D),
            whole(ROWS, D),
            whole(ROWS, 128),
            whole(8, D),
            whole(ROWS, D),
        ],
        out_shape=[
            jax.ShapeDtypeStruct((ROWS, D), BF16),
            jax.ShapeDtypeStruct((ROWS, FF), BF16),
            jax.ShapeDtypeStruct((ROWS, FF), BF16),
            jax.ShapeDtypeStruct((ROWS, FF), BF16),
            jax.ShapeDtypeStruct((ROWS, D), BF16),
            jax.ShapeDtypeStruct((ROWS, D), F32),
            jax.ShapeDtypeStruct((ROWS, 128), F32),
            jax.ShapeDtypeStruct((8, D), F32),
            jax.ShapeDtypeStruct((ROWS, D), BF16),
        ],
        compiler_params=pltpu.CompilerParams(vmem_limit_bytes=VMEM_LIMIT),
        name="feed",
    )(h1, x, t, aux, gain, router, *packs)


def down_grad_kernel(hid_ref, d_ffn_ref, out_ref):
    out_ref[...] = tn(hid_ref[...], d_ffn_ref[...]).astype(BF16)


def down_grad(hid, d_ffn):
    return pl.pallas_call(
        down_grad_kernel,
        grid=(FF // CHUNK,),
        in_specs=[
            pl.BlockSpec((ROWS, CHUNK), lambda j: (0, j)),
            pl.BlockSpec((ROWS, D), lambda j: (0, 0)),
        ],
        out_specs=pl.BlockSpec((CHUNK, D), lambda j: (j, 0)),
        out_shape=jax.ShapeDtypeStruct((FF, D), BF16),
        compiler_params=pltpu.CompilerParams(vmem_limit_bytes=VMEM_LIMIT),
        name="down_grad",
    )(hid, d_ffn)


def feed_back_kernel(
    h1_ref, n2_ref, diff_ref, cols_ref, gain_ref, router_ref, g_ref, u_ref, d_ffn_ref,
    wg_ref, wu_ref, wd_ref,
    ggu_ref, da_ref, part_ref, sums_ref,
    d_gate, d_up,
):
    step = pl.program_id(0)

    @pl.when(step == 0)
    def _():
        part_ref[...] = jnp.zeros_like(part_ref)

    for start in range(0, SLAB, CHUNK):
        span = slice(start, start + CHUNK)
        d_hidden = nt(d_ffn_ref[...], rows_of(wd_ref, start, CHUNK))
        gate = g_ref[:, span].astype(F32)
        up = u_ref[:, span].astype(F32)
        sig = jax.nn.sigmoid(gate)
        d_gate[:, span] = (d_hidden * up * sig * (1.0 + gate * (1.0 - sig))).astype(BF16)
        d_up[:, span] = (d_hidden * gate * sig).astype(BF16)
        ggu_ref[0, span] = tn(d_gate[:, span], n2_ref[...]).astype(BF16)
        ggu_ref[1, span] = tn(d_up[:, span], n2_ref[...]).astype(BF16)
    part_ref[...] += nn(d_gate[...], rows_of(wg_ref)) + nn(d_up[...], rows_of(wu_ref))

    @pl.when(step == pl.num_programs(0) - 1)
    def _():
        h1 = h1_ref[...]
        inv = lax.rsqrt(jnp.mean(h1 * h1, axis=-1, keepdims=True) + EPS)
        d_norm = part_ref[...]
        sums_ref[...] = jnp.broadcast_to(
            jnp.sum(d_norm * h1 * inv, axis=0, keepdims=True), sums_ref.shape
        )
        scaled = d_norm * gain_ref[...]
        d_inner = inv * scaled - h1 * inv**3 * jnp.mean(scaled * h1, axis=-1, keepdims=True)
        diff = diff_ref[...]
        da_ref[...] = (cols_ref[:, 0:1] * diff + d_inner).astype(BF16)
        part_ref[...] = diff + cols_ref[:, 1:2] * router_ref[...] + d_inner


def feed_back(h1, n2, diff, cols, gain, router, g, u, d_ffn, packs):
    whole = lambda *shape: pl.BlockSpec(shape, lambda j: (0,) * len(shape))
    fixed = lambda *shape: pl.BlockSpec(
        shape, lambda j: (0,) * len(shape), pipeline_mode=pl.Buffered(1)
    )
    return pl.pallas_call(
        feed_back_kernel,
        grid=(FF // SLAB,),
        in_specs=[
            fixed(ROWS, D),
            fixed(ROWS, D),
            fixed(ROWS, D),
            fixed(ROWS, 128),
            fixed(1, D),
            fixed(1, D),
            pl.BlockSpec((ROWS, SLAB), lambda j: (0, j)),
            pl.BlockSpec((ROWS, SLAB), lambda j: (0, j)),
            fixed(ROWS, D),
            *feed_specs(packs),
        ],
        out_specs=[
            pl.BlockSpec((2, SLAB, D), lambda j: (0, j, 0)),
            whole(ROWS, D),
            whole(ROWS, D),
            whole(8, D),
        ],
        out_shape=[
            jax.ShapeDtypeStruct((2, FF, D), BF16),
            jax.ShapeDtypeStruct((ROWS, D), BF16),
            jax.ShapeDtypeStruct((ROWS, D), F32),
            jax.ShapeDtypeStruct((8, D), F32),
        ],
        scratch_shapes=[
            pltpu.VMEM((ROWS, SLAB), BF16),
            pltpu.VMEM((ROWS, SLAB), BF16),
        ],
        compiler_params=pltpu.CompilerParams(vmem_limit_bytes=VMEM_LIMIT),
        name="feed_back",
    )(h1, n2, diff, cols, gain, router, g, u, d_ffn, *packs)


def attend_back_kernel(
    final, da_ref, part_ref, x_ref, n1_ref, gain_ref, cos_ref, sin_ref, aux_ref, row_ref,
    q_ref, k_ref, v_ref, o_ref, l_ref, wq_ref, wk_ref, wv_ref, wo0_ref, wo1_ref, wo2_ref,
    sofar_ref, _gq, _gk, _gv, _go,
    gq_ref, gk_ref, gv_ref, go_ref, dn1, grad_ref, sums_ref,
    bias, wide_q, wide_do, dq,
):
    group = pl.program_id(0)
    per = D // KV_HEADS

    @pl.when(group == 0)
    def _():
        bias[...] = jnp.where(aux_ref[:, 3:4] <= row_ref[0:1, :], 0.0, NEG)
        wide_q[...] = jnp.zeros_like(wide_q)
        wide_do[...] = jnp.zeros_like(wide_do)
        dn1[...] = sofar_ref[...]

    w_out = jnp.concatenate([wo0_ref[...], wo1_ref[...], wo2_ref[...]], axis=0)
    d_heads = nt(da_ref[...], w_out)
    d_low = d_heads.astype(BF16)
    go_ref[...] = tn(o_ref[0], da_ref[...]).astype(BF16)
    both = d_low.astype(F32) * o_ref[0].astype(F32)
    key, value = k_ref[0], v_ref[0]
    d_key = jnp.zeros((ROWS, HEAD), F32)
    d_value = jnp.zeros((ROWS, HEAD), F32)
    d_queries = []
    ones = jnp.ones((8, HEAD), F32)
    for head in range(PER_KV):
        span = slice(head * HEAD, (head + 1) * HEAD)
        wide_q[:ROWS] = q_ref[head]
        wide_do[:ROWS] = d_low[:, span]
        inside = lax.dot_general(
            ones, both[:, span], (((1,), (1,)), ((), ())),
            preferred_element_type=F32, precision=lax.Precision.HIGHEST,
        )
        inside = jnp.concatenate([inside, jnp.zeros((8, WIDE - ROWS), F32)], axis=1)
        for start, stop, reach in TILES:
            end = start + TILE
            reach = min(reach, ROWS)
            scores = nt(key[:reach], wide_q[start:end]) * 0.125 + bias[:reach, start:end]
            probs = jnp.exp(scores - l_ref[0, head : head + 1, start:end])
            d_probs = nt(value[:reach], wide_do[start:end])
            d_scores = (probs * (d_probs - inside[0:1, start:end])).astype(BF16)
            add_k = nn(d_scores, wide_q[start:end])
            add_v = nn(probs.astype(BF16), wide_do[start:end])
            if reach < ROWS:
                rest = jnp.zeros((ROWS - reach, HEAD), F32)
                add_k = jnp.concatenate([add_k, rest], axis=0)
                add_v = jnp.concatenate([add_v, rest], axis=0)
            d_key += add_k
            d_value += add_v
            dq[start:end] = tn(d_scores, key[:reach]) * 0.125
        d_queries.append(dq[:ROWS])
    turned_back = turned(
        jnp.concatenate(d_queries + [d_key * 0.125], axis=1), cos_ref[...], -sin_ref[...]
    )
    d_mixed = jnp.concatenate(turned_back + [d_value], axis=1).astype(BF16)
    grads = tn(d_mixed, n1_ref[...]).astype(BF16)
    gq_ref[...] = grads[:per]
    gk_ref[...] = grads[per : per + HEAD]
    gv_ref[...] = grads[per + HEAD :]
    packed = jnp.concatenate([wq_ref[...], wk_ref[...], wv_ref[...]], axis=0)
    dn1[...] += nn(d_mixed, packed)

    if not final:
        return

    @pl.when(group == pl.num_programs(0) - 1)
    def _():
        x = x_ref[...].astype(F32)
        inv = lax.rsqrt(jnp.mean(x * x, axis=-1, keepdims=True) + EPS)
        d_norm = dn1[...]
        sums_ref[...] = jnp.broadcast_to(
            jnp.sum(d_norm * x * inv, axis=0, keepdims=True), sums_ref.shape
        )
        scaled = d_norm * gain_ref[...]
        d_x = inv * scaled - x * inv**3 * jnp.mean(scaled * x, axis=-1, keepdims=True)
        grad_ref[...] = (part_ref[...] + d_x).astype(BF16)


def attend_back(first, count, given, so_far):
    whole = lambda *shape: pl.BlockSpec(shape, lambda g: (0,) * len(shape))
    fixed = lambda *shape: pl.BlockSpec(
        shape, lambda g: (0,) * len(shape), pipeline_mode=pl.Buffered(1)
    )
    per = D // KV_HEADS
    final = first + count == KV_HEADS
    kept = pl.BlockSpec(memory_space=pl.ANY)
    return pl.pallas_call(
        functools.partial(attend_back_kernel, final),
        grid=(count,),
        in_specs=[
            fixed(ROWS, D),
            fixed(ROWS, D),
            fixed(ROWS, D),
            fixed(ROWS, D),
            fixed(1, D),
            fixed(ROWS, HEAD),
            fixed(ROWS, HEAD),
            fixed(ROWS, 8),
            fixed(8, WIDE),
            pl.BlockSpec((PER_KV, ROWS, HEAD), lambda g: (first + g, 0, 0)),
            pl.BlockSpec((1, ROWS, HEAD), lambda g: (first + g, 0, 0)),
            pl.BlockSpec((1, ROWS, HEAD), lambda g: (first + g, 0, 0)),
            pl.BlockSpec((1, ROWS, per), lambda g: (first + g, 0, 0)),
            pl.BlockSpec((1, 8, WIDE), lambda g: (first + g, 0, 0)),
            *weight_specs(first),
            fixed(ROWS, D),
            kept,
            kept,
            kept,
            kept,
        ],
        out_specs=[
            pl.BlockSpec((per, D), lambda g: (first + g, 0)),
            pl.BlockSpec((HEAD, D), lambda g: (first + g, 0)),
            pl.BlockSpec((HEAD, D), lambda g: (first + g, 0)),
            pl.BlockSpec((per, D), lambda g: (first + g, 0)),
            whole(ROWS, D),
            whole(ROWS, D),
            whole(8, D),
        ],
        out_shape=[
            jax.ShapeDtypeStruct((D, D), BF16),
            jax.ShapeDtypeStruct((KV_WIDTH, D), BF16),
            jax.ShapeDtypeStruct((KV_WIDTH, D), BF16),
            jax.ShapeDtypeStruct((D, D), BF16),
            jax.ShapeDtypeStruct((ROWS, D), F32),
            jax.ShapeDtypeStruct((ROWS, D), BF16),
            jax.ShapeDtypeStruct((8, D), F32),
        ],
        scratch_shapes=[
            pltpu.VMEM((ROWS, WIDE), F32),
            pltpu.VMEM((WIDE, HEAD), BF16),
            pltpu.VMEM((WIDE, HEAD), BF16),
            pltpu.VMEM((WIDE, HEAD), F32),
        ],
        input_output_aliases={21: 0, 22: 1, 23: 2, 24: 3},
        compiler_params=pltpu.CompilerParams(vmem_limit_bytes=VMEM_LIMIT),
        name="attend_back",
    )(*given, *so_far)


def on_device(states, teacher, validity, chosen, attn_pack, gate_up, down_proj, norm_gains, router):
    seq_count, block_rows, width = states.shape
    ctx_count = lax.axis_size("ctx")
    if seq_count != ctx_count:
        raise ValueError("seq_count")
    seq_length = block_rows * ctx_count
    bits = device_bits()
    gain_one, gain_two = norm_gains[0:1], norm_gains[1:2]

    flags = to_sequence((validity + 2 * chosen).reshape(seq_count, 1, block_rows))
    x_seq = to_sequence(states).reshape(seq_length, width)
    feed_rows = jnp.concatenate([gate_up.T, down_proj.T], axis=0)
    packs = lax.all_gather(feed_rows, ("dp", "ctx"), axis=0)
    w_low, w_high = gather_halves(attn_pack.T, bits)
    teacher_late, w_low, w_high = join(teacher, w_low, w_high)
    t_seq = to_sequence(teacher_late).reshape(seq_length, width)
    thin = down_proj.shape[1]
    if thin % 16:
        wide = packs[:, : 2 * thin].reshape(2 * FF, width)
        packs = (wide, wide, packs[:, 2 * thin :].reshape(FF, width))
    else:
        packs = (packs, packs, packs)

    flags = flags.reshape(seq_length)
    chosen_seq, valid_seq = flags >> 1, flags & 1
    place = jnp.arange(seq_length)
    rank = jnp.sum(jnp.where(place[:, None] < place[None, :], chosen_seq[:, None], 0), axis=0)
    slot = jnp.where(chosen_seq > 0, rank, -1)
    pick = (jnp.arange(ROWS)[:, None] == slot[None, :]).astype(BF16)
    picked = pick.astype(F32)
    pos = jnp.sum(picked * place.astype(F32)[None, :], axis=1)
    valid = jnp.sum(picked * valid_seq.astype(F32)[None, :], axis=1)
    live = (jnp.arange(ROWS) < jnp.sum(chosen_seq)).astype(F32)

    x_low = dot(pick, x_seq, ((1,), (0,))).astype(BF16)
    t_low = dot(pick, t_seq, ((1,), (0,))).astype(BF16)

    half = HEAD // 2
    freqs = THETA ** (-(jnp.arange(half).astype(F32) * 2.0 / HEAD))
    angles = pos[:, None] * freqs[None, :]
    cosine, sine = jnp.cos(angles), jnp.sin(angles)
    cosine = jnp.concatenate([cosine, cosine], axis=1)
    sine = jnp.concatenate([-sine, sine], axis=1)
    block = jnp.floor(pos / block_rows)
    key_block = jnp.where(valid * live > 0.5, block, 1e6)
    aux = jnp.stack([valid, live, block, key_block] + [jnp.zeros_like(pos)] * 4, axis=1)
    row = jnp.stack([block, key_block] + [jnp.zeros_like(pos)] * 6, axis=0)
    row = jnp.pad(row, ((0, 0), (0, WIDE - ROWS)), constant_values=1e6)
    router_row = router[None, :]

    n1, q, k, v, o, lse, h1 = attend(x_low, gain_one, cosine, sine, aux, row, w_low, w_high)
    n2, g, u, hid, y, diff, cols, sums, d_ffn = feed(
        h1, x_low, t_low, aux, gain_two, router_row, packs
    )
    energy = jnp.sum(sums[1])

    def to_home(compact):
        whole = dot(pick, compact, ((0,), (0,))).astype(BF16)
        return to_sequence(whole.reshape(ctx_count, block_rows, width))

    out_home = to_home(y)
    down_half = down_grad(hid, d_ffn).reshape(2, FF // 2, width)
    down = Scatter([down_half[0], down_half[1]], bits)
    got = down.send()
    got = join(*got)
    down.take(got)
    got = down.send()
    grad_gu, da, part, two = feed_back(
        h1, n2, diff, cols, gain_two, router_row, g, u, d_ffn, packs
    )
    da, out_home, *got = join(da, out_home, *got)
    down.take(got)
    wide = Scatter([grad_gu[0], grad_gu[1]], bits)
    got, got_wide = down.send(), wide.send()

    given = (da, part, x_low, n1, gain_one, cosine, sine, aux, row, q, k, v, o, lse)
    given += (w_low, w_low, w_high, w_high, w_high, w_high)
    room = [jnp.zeros((D, width), BF16), jnp.zeros((KV_WIDTH, width), BF16)]
    so_far = [jnp.zeros((ROWS, width), F32), room[0], room[1], room[1], room[0]]
    down.got, wide.got = got, got_wide
    for first, count in ((0, 2), (2, 2), (4, 1)):
        gq, gk, gv, go, dn1, d_states, one = attend_back(first, count, given, so_far)
        dn1 = advance([down, wide], dn1)
        so_far = [dn1, gq, gk, gv, go]
    attn = Scatter(
        [jnp.concatenate([gq, gk], axis=0), jnp.concatenate([gv, go], axis=0)], bits
    )
    grad_home = to_home(d_states)
    attn.got = attn.send()
    while attn.part is None or wide.part is None or down.part is None:
        advance([attn, wide, down], None)
    attn_part, gu_part, down_part = attn.part, wide.part, down.part
    grad_gain_one, grad_gain_two, grad_router = one[0], two[0], sums[0]

    x_home = states.astype(F32)
    still = (chosen == 0)[..., None]
    valid_home = validity.astype(F32)[..., None]
    apart = valid_home * (x_home - teacher.astype(F32))
    energy = energy + 0.5 * jnp.sum(jnp.where(still, apart * apart, 0.0))
    states_out = jnp.where(still, states, out_home)
    states_grad = jnp.where(still, apart, grad_home.astype(F32))

    scalars = jnp.concatenate(
        [energy[None], jnp.sum(validity).astype(F32)[None], jnp.zeros((D - 2,), F32)]
    )
    small = jnp.stack([grad_gain_one, grad_gain_two, grad_router, scalars], axis=0)
    small = all_sum(small, bits)
    mse_loss = 2.0 * small[3, 0] / (small[3, 1] * D)
    return (
        states_out,
        mse_loss,
        states_grad,
        attn_part.T,
        gu_part.T,
        down_part.T,
        small[0:2],
        small[2],
    )


def solution(mesh):
    tokens = P("dp", "ctx", None)
    flags = P("dp", "ctx")
    packs = P(None, ("dp", "ctx"))
    return jax.shard_map(
        on_device,
        mesh=mesh,
        in_specs=(tokens, tokens, flags, flags, packs, packs, packs, P(), P()),
        out_specs=(tokens, P(), tokens, packs, packs, packs, P(), P()),
        check_vma=False,
    )
```

```python
import functools

import jax
import jax.numpy as jnp
from jax import lax
from jax.experimental import pallas as pl
from jax.experimental.pallas import tpu as pltpu
from jax.sharding import PartitionSpec as P

D = 960
HEADS = 15
KV_HEADS = 5
HEAD = 64
FF = 2560
CHOSEN = 640
PER_KV = HEADS // KV_HEADS
KV_WIDTH = KV_HEADS * HEAD
QKV_COLS = D + 2 * KV_WIDTH
ROWS = 656
TILE = 256
WIDE = 768
SLAB = 1280
SPLIT = ((0, 2), (2, 2), (4, 1))
CHUNK = 640
TILES = ((0, 256, 512), (256, 512, 768), (512, ROWS, 768))
NEG = -1e30
VMEM_LIMIT = 62 * 1024 * 1024

EPS = 1e-05
THETA = 10000.0
F32 = jnp.float32
BF16 = jnp.bfloat16


def device_bits():
    found = []
    for name in ("dp", "ctx"):
        count = lax.axis_size(name)
        found += [(name, bit) for bit in reversed(range(count.bit_length() - 1))]
    return found


def swap(value, place):
    name, bit = place
    pairs = [(i, i ^ (1 << bit)) for i in range(lax.axis_size(name))]
    return lax.ppermute(value, name, pairs)


def own_bit(place):
    name, bit = place
    return (lax.axis_index(name) >> bit) & 1


def routes(bits):
    count = len(bits)
    far = list(range(1, count - 3))
    return [far + [count - 3, count - 2, count - 1], far + [count - 2, count - 3, count - 1]]


def late_routes(bits):
    count = len(bits)
    far = list(range(count - 4, 0, -1))
    return [[count - 3] + far + [count - 2], far + [count - 3, count - 2]]


def join(*values):
    return lax.optimization_barrier(values)


def own_bits(bits):
    return jnp.stack([own_bit(place) for place in bits]).astype(jnp.int32)


def order_kernel(spots, own, mine0, other0, mine1, other1, out, sems):
    last = len(spots[0])

    def copies(place):
        found = []
        for half, (mine, other) in enumerate(((mine0, other0), (mine1, other1))):
            slot = 0
            for level, spot in enumerate(spots[half]):
                slot = slot + ((((place >> level) & 1) ^ own[spot]) << (last - spot))
            core = own[last + 1]
            for k, (source, side) in enumerate(((mine, core), (other, 1 - core))):
                found.append(
                    pltpu.make_async_copy(
                        source.at[place], out.at[half, slot, side], sems.at[2 * half + k, place]
                    )
                )
        return found

    def begin(place, carry):
        for copy in copies(place):
            copy.start()
        return carry

    def end(place, carry):
        for copy in copies(place):
            copy.wait()
        return carry

    count = mine0.shape[0]
    lax.fori_loop(0, count, begin, 0)
    lax.fori_loop(0, count, end, 0)


class Gather:
    def __init__(self, shard, bits):
        self.bits = bits
        self.halves, self.routes = [shard[None]], routes(bits)
        self.step, self.part = 0, None
        self.got = []

    def send(self):
        if self.step == 0:
            self.got = [swap(self.halves[0], self.bits[0])]
        else:
            spots = [route[self.step - 1] for route in self.routes]
            self.got = [swap(h, self.bits[s]) for h, s in zip(self.halves, spots)]
        self.step += 1

    def take(self):
        if self.step == 1:
            low_side = own_bit(self.bits[0]) == 0
            shard, other = self.halves[0], self.got[0]
            self.halves = [jnp.where(low_side, shard, other), jnp.where(low_side, other, shard)]
        elif self.step < len(self.bits):
            self.halves = [jnp.concatenate(p, axis=0) for p in zip(self.halves, self.got)]
        else:
            self.part = self.ordered()

    def ordered(self):
        count, rows, width = self.halves[0].shape
        anywhere = pl.BlockSpec(memory_space=pl.ANY)
        out = pl.pallas_call(
            functools.partial(order_kernel, [r[:-1] for r in self.routes]),
            in_specs=[pl.BlockSpec(memory_space=pltpu.SMEM)] + [anywhere] * 4,
            out_specs=pl.BlockSpec(memory_space=pltpu.VMEM),
            out_shape=jax.ShapeDtypeStruct((2, count, 2, rows, width), BF16),
            scratch_shapes=[pltpu.SemaphoreType.DMA((4, count))],
            compiler_params=pltpu.CompilerParams(vmem_limit_bytes=VMEM_LIMIT),
            name="order",
        )(own_bits(self.bits), self.halves[0], self.got[0], self.halves[1], self.got[1])
        return out.reshape(-1, width)


class Scatter:
    def __init__(self, keep, send, bits, late=False):
        self.bits = bits
        self.keep, self.out = keep, send
        self.routes = late_routes(bits) if late else [route[-2::-1] for route in routes(bits)]
        self.step, self.part = 0, None
        self.got, self.outs = [], []

    def choose(self, half, choice):
        total = 0.0
        for array, held in self.parts[half]:
            rows, width = array.shape[-2:]
            run = [h for h in held if h in choice]
            if run:
                at, index = held.index(run[0]), 0
                for spot in run:
                    index = 2 * index + choice[spot]
                cube = array.reshape(1 << at, 1 << len(run), -1, width)
                array = lax.dynamic_index_in_dim(cube, index, 1, keepdims=False)
            total = total + array.reshape(-1, rows, width).astype(F32)
        return total

    def cut(self):
        last = len(self.bits) - 1
        if self.step == 0:
            self.outs, self.spots = [self.out], [last]
        elif self.step < last:
            self.outs, self.spots = [], []
            for half, route in enumerate(self.routes):
                choice = {s: own_bit(self.bits[s]) for s in route[: self.step]}
                spot = route[self.step - 1]
                choice[spot] = 1 - choice[spot]
                self.outs.append(self.choose(half, choice).astype(BF16))
                self.spots.append(spot)
        else:
            low_side = own_bit(self.bits[0]) == 0
            sums = []
            for half, route in enumerate(self.routes):
                sums.append(self.choose(half, {s: own_bit(self.bits[s]) for s in route})[0])
            self.mine = jnp.where(low_side, sums[0], sums[1])
            self.outs = [jnp.where(low_side, sums[1], sums[0]).astype(BF16)]
            self.spots = [0]

    def send(self):
        if not self.outs:
            self.cut()
        self.got = [swap(out, self.bits[spot]) for out, spot in zip(self.outs, self.spots)]
        self.outs = []
        self.step += 1

    def take(self):
        if self.step == 1:
            held = sorted(self.routes[0])
            self.parts = [
                [(self.keep[half], held), (self.got[0][half], held)] for half in range(2)
            ]
        elif self.step <= len(self.bits) - 1:
            for parts, got, route in zip(self.parts, self.got, self.routes):
                parts.append((got, sorted(route[self.step - 1 :])))
        else:
            self.part = self.mine + self.got[0].astype(F32)


def split_cores(whole, bits):
    count = 1 << (len(bits) - 2)
    cube = whole.reshape(2 * count, 2, -1, whole.shape[-1])
    mine = own_bit(bits[-1])
    both = [lax.dynamic_index_in_dim(cube, side, 1, keepdims=False) for side in (mine, 1 - mine)]
    return [b.reshape(2, count, -1, whole.shape[-1]) for b in both]


def start(*moves):
    for m in moves:
        if m.part is None and not m.got:
            m.send()


def start_ahead(moves, *values):
    moves = [m for m in moves if m.part is None and not m.got]
    for m in moves:
        m.cut()
    flat = list(join(*values, *[o for m in moves for o in m.outs]))
    values, flat = flat[: len(values)], flat[len(values) :]
    for m in moves:
        m.outs, flat = flat[: len(m.outs)], flat[len(m.outs) :]
        m.send()
    return values if len(values) != 1 else values[0]


def take(*moves):
    for m in moves:
        if m.got:
            m.take()
            m.got = []


def wait(moves, *values):
    moves = [m for m in moves if m.got]
    flat = list(join(*values, *[g for m in moves for g in m.got]))
    values, flat = flat[: len(values)], flat[len(values) :]
    for m in moves:
        m.got, flat = flat[: len(m.got)], flat[len(m.got) :]
    take(*moves)
    return values if len(values) != 1 else values[0]


def finish(*moves):
    while any(m.part is None for m in moves):
        start(*moves)
        take(*moves)


class Total:
    def __init__(self, value, bits):
        self.value, self.bits = value, bits
        self.step, self.part, self.got = 0, None, []

    def send(self):
        self.got = [swap(self.value, self.bits[self.step])]
        self.step += 1

    def take(self):
        self.value = self.value + self.got[0]
        if self.step == len(self.bits):
            self.part = self.value


def dot(left, right, contract):
    return lax.dot_general(left, right, (contract, ((), ())), preferred_element_type=F32)


def to_sequence(blocks):
    return lax.all_to_all(blocks, "ctx", split_axis=0, concat_axis=0, tiled=True)


def nt(left, right):
    return lax.dot_general(left, right, (((1,), (1,)), ((), ())), preferred_element_type=F32)


def nn(left, right):
    return lax.dot_general(left, right, (((1,), (0,)), ((), ())), preferred_element_type=F32)


def tn(left, right):
    return lax.dot_general(left, right, (((0,), (0,)), ((), ())), preferred_element_type=F32)


def turned(values, cosine, sine):
    half = HEAD // 2
    pieces = []
    for start in range(0, values.shape[1], HEAD):
        head = values[:, start : start + HEAD]
        swapped = jnp.concatenate([head[:, half:], head[:, :half]], axis=1)
        pieces.append(head * cosine + swapped * sine)
    return pieces


def weight_specs(first):
    places = [HEADS, HEADS + KV_HEADS] + [QKV_COLS // HEAD + r for r in range(PER_KV)]
    steps = [1, 1] + [PER_KV] * PER_KV
    return [pl.BlockSpec((D // KV_HEADS, D), lambda g: (first + g, 0))] + [
        pl.BlockSpec((HEAD, D), lambda g, p=p, s=s: (p + s * (first + g), 0))
        for p, s in zip(places, steps)
    ]


def attend_kernel(
    x_ref, gain_ref, cos_ref, sin_ref, aux_ref, row_ref, wq_ref, wk_ref, wv_ref, wo0_ref, wo1_ref, wo2_ref,
    n1_ref, q_ref, k_ref, v_ref, o_ref, l_ref, h1_ref,
    bias, keys, vals, lse,
):
    group = pl.program_id(0)

    @pl.when(group == 0)
    def _():
        x = x_ref[...].astype(F32)
        inv = lax.rsqrt(jnp.mean(x * x, axis=-1, keepdims=True) + EPS)
        n1_ref[...] = (x * inv * gain_ref[...]).astype(BF16)
        h1_ref[...] = x
        bias[...] = jnp.where(row_ref[1:2, :] <= aux_ref[:, 2:3], 0.0, NEG)
        keys[...] = jnp.zeros_like(keys)
        vals[...] = jnp.zeros_like(vals)
        lse[...] = jnp.zeros_like(lse)

    packed = jnp.concatenate([wq_ref[...], wk_ref[...], wv_ref[...]], axis=0)
    mixed = nt(n1_ref[...], packed)
    rotated = turned(mixed[:, : D // KV_HEADS + HEAD], cos_ref[...], sin_ref[...])
    key = rotated[PER_KV].astype(BF16)
    value = mixed[:, D // KV_HEADS + HEAD :].astype(BF16)
    k_ref[0] = key
    v_ref[0] = value
    keys[:ROWS] = key
    vals[:ROWS] = value
    for head in range(PER_KV):
        q_ref[head] = rotated[head].astype(BF16)
    lanes = lax.broadcasted_iota(jnp.int32, (1, 128), 1)
    for start, stop, reach in TILES:
        outs = []
        logs = jnp.zeros((stop - start, 128), F32)
        for head in range(PER_KV):
            scores = nt(q_ref[head, start:stop], keys[:reach]) * 0.125 + bias[start:stop, :reach]
            top = jnp.max(scores, axis=-1, keepdims=True)
            expd = jnp.exp(scores - top)
            total = jnp.sum(expd, axis=-1, keepdims=True)
            outs.append(nn(expd.astype(BF16), vals[:reach]) / total)
            logs = jnp.where(lanes == head, top + jnp.log(total), logs)
        o_ref[0, start:stop] = jnp.concatenate(outs, axis=1).astype(BF16)
        lse[start:stop] = logs
    l_ref[0] = lse[...].T[:8]
    h1_ref[...] += nn(o_ref[0], jnp.concatenate([wo0_ref[...], wo1_ref[...], wo2_ref[...]], axis=0))


def attend(x, gain, cosine, sine, aux, row, w_attn):
    whole = lambda *shape: pl.BlockSpec(shape, lambda g: (0,) * len(shape))
    fixed = lambda *shape: pl.BlockSpec(
        shape, lambda g: (0,) * len(shape), pipeline_mode=pl.Buffered(1)
    )
    per = D // KV_HEADS
    return pl.pallas_call(
        attend_kernel,
        grid=(KV_HEADS,),
        in_specs=[
            fixed(ROWS, D),
            fixed(1, D),
            fixed(ROWS, HEAD),
            fixed(ROWS, HEAD),
            fixed(ROWS, 8),
            fixed(8, WIDE),
            *weight_specs(0),
        ],
        out_specs=[
            whole(ROWS, D),
            pl.BlockSpec((PER_KV, ROWS, HEAD), lambda g: (g, 0, 0)),
            pl.BlockSpec((1, ROWS, HEAD), lambda g: (g, 0, 0)),
            pl.BlockSpec((1, ROWS, HEAD), lambda g: (g, 0, 0)),
            pl.BlockSpec((1, ROWS, per), lambda g: (g, 0, 0)),
            pl.BlockSpec((1, 8, WIDE), lambda g: (g, 0, 0)),
            whole(ROWS, D),
        ],
        out_shape=[
            jax.ShapeDtypeStruct((ROWS, D), BF16),
            jax.ShapeDtypeStruct((HEADS, ROWS, HEAD), BF16),
            jax.ShapeDtypeStruct((KV_HEADS, ROWS, HEAD), BF16),
            jax.ShapeDtypeStruct((KV_HEADS, ROWS, HEAD), BF16),
            jax.ShapeDtypeStruct((KV_HEADS, ROWS, per), BF16),
            jax.ShapeDtypeStruct((KV_HEADS, 8, WIDE), F32),
            jax.ShapeDtypeStruct((ROWS, D), F32),
        ],
        scratch_shapes=[
            pltpu.VMEM((ROWS, WIDE), F32),
            pltpu.VMEM((WIDE, HEAD), BF16),
            pltpu.VMEM((WIDE, HEAD), BF16),
            pltpu.VMEM((WIDE, 128), F32),
        ],
        compiler_params=pltpu.CompilerParams(vmem_limit_bytes=VMEM_LIMIT),
        name="attend",
    )(x, gain, cosine, sine, aux, row, *[w_attn] * 6)


def feed_specs(packs):
    if packs[0].ndim == 2:
        return [
            pl.BlockSpec((SLAB, D), lambda j: (j, 0)),
            pl.BlockSpec((SLAB, D), lambda j: (FF // SLAB + j, 0)),
            pl.BlockSpec((SLAB, D), lambda j: (j, 0)),
        ]
    count, rows, _ = packs[0].shape
    thin = rows // 3
    return [
        pl.BlockSpec((SLAB // (2 * thin), 2 * thin, D), lambda j: (j, 0, 0)),
        pl.BlockSpec((SLAB // (2 * thin), 2 * thin, D), lambda j: (FF // SLAB + j, 0, 0)),
        pl.BlockSpec((SLAB // thin, thin, D), lambda j: (j, 2, 0)),
    ]


def rows_of(ref, start=0, size=SLAB):
    if len(ref.shape) == 2:
        return ref[start : start + size]
    each = ref.shape[1]
    return ref[start // each : (start + size) // each].reshape(size, D)


def feed_kernel(
    h1_ref, x_ref, t_ref, aux_ref, gain_ref, router_ref, wg_ref, wu_ref, wd_ref,
    n2_ref, g_ref, u_ref, hid_ref, y_ref, diff_ref, cols_ref, sums_ref, d_ffn_ref,
):
    step = pl.program_id(0)

    @pl.when(step == 0)
    def _():
        h1 = h1_ref[...]
        inv = lax.rsqrt(jnp.mean(h1 * h1, axis=-1, keepdims=True) + EPS)
        n2_ref[...] = (h1 * inv * gain_ref[...]).astype(BF16)
        diff_ref[...] = h1 - x_ref[...].astype(F32)

    for start in range(0, SLAB, CHUNK):
        span = slice(start, start + CHUNK)
        gate = nt(n2_ref[...], rows_of(wg_ref, start, CHUNK))
        up = nt(n2_ref[...], rows_of(wu_ref, start, CHUNK))
        g_ref[:, span] = gate.astype(BF16)
        u_ref[:, span] = up.astype(BF16)
        hid_ref[:, span] = (gate * jax.nn.sigmoid(gate) * up).astype(BF16)
    diff_ref[...] += nn(hid_ref[...], rows_of(wd_ref))

    @pl.when(step == pl.num_programs(0) - 1)
    def _():
        x = x_ref[...].astype(F32)
        branch = diff_ref[...]
        valid, live = aux_ref[:, 0:1], aux_ref[:, 1:2]
        prob = jax.nn.sigmoid(jnp.sum(x * router_ref[...], axis=-1, keepdims=True))
        mix = live * prob
        result = x + mix * branch
        y_ref[...] = result.astype(BF16)
        diff = valid * (result - t_ref[...].astype(F32))
        d_logit = live * jnp.sum(diff * branch, axis=-1, keepdims=True) * prob * (1.0 - prob)
        diff_ref[...] = diff
        d_ffn_ref[...] = (mix * diff).astype(BF16)
        lanes = lax.broadcasted_iota(jnp.int32, (1, 128), 1)
        cols_ref[...] = jnp.where(lanes == 0, mix, jnp.where(lanes == 1, d_logit, 0.0))
        sums_ref[...] = jnp.concatenate(
            [
                jnp.sum(d_logit * x, axis=0, keepdims=True),
                0.5 * jnp.sum(diff * diff, axis=0, keepdims=True),
                jnp.zeros((6, D), F32),
            ],
            axis=0,
        )


def feed(h1, x, t, aux, gain, router, packs):
    whole = lambda *shape: pl.BlockSpec(shape, lambda j: (0,) * len(shape))
    fixed = lambda *shape: pl.BlockSpec(
        shape, lambda j: (0,) * len(shape), pipeline_mode=pl.Buffered(1)
    )
    return pl.pallas_call(
        feed_kernel,
        grid=(FF // SLAB,),
        in_specs=[
            fixed(ROWS, D),
            fixed(ROWS, D),
            fixed(ROWS, D),
            fixed(ROWS, 8),
            fixed(1, D),
            fixed(1, D),
            *feed_specs(packs),
        ],
        out_specs=[
            whole(ROWS, D),
            pl.BlockSpec((ROWS, SLAB), lambda j: (0, j)),
            pl.BlockSpec((ROWS, SLAB), lambda j: (0, j)),
            pl.BlockSpec((ROWS, SLAB), lambda j: (0, j)),
            whole(ROWS, D),
            whole(ROWS, D),
            whole(ROWS, 128),
            whole(8, D),
            whole(ROWS, D),
        ],
        out_shape=[
            jax.ShapeDtypeStruct((ROWS, D), BF16),
            jax.ShapeDtypeStruct((ROWS, FF), BF16),
            jax.ShapeDtypeStruct((ROWS, FF), BF16),
            jax.ShapeDtypeStruct((ROWS, FF), BF16),
            jax.ShapeDtypeStruct((ROWS, D), BF16),
            jax.ShapeDtypeStruct((ROWS, D), F32),
            jax.ShapeDtypeStruct((ROWS, 128), F32),
            jax.ShapeDtypeStruct((8, D), F32),
            jax.ShapeDtypeStruct((ROWS, D), BF16),
        ],
        compiler_params=pltpu.CompilerParams(vmem_limit_bytes=VMEM_LIMIT),
        name="feed",
    )(h1, x, t, aux, gain, router, *packs)


def shared_out(core_ref, total, refs, rows):
    low = core_ref[0] == 0
    for pair in range(total.shape[0] // (2 * rows)):
        even = total[2 * pair * rows : (2 * pair + 1) * rows]
        odd = total[(2 * pair + 1) * rows : (2 * pair + 2) * rows]
        refs[0][pair] = jnp.where(low, even, odd).astype(BF16)
        refs[1][pair] = jnp.where(low, odd, even).astype(BF16)


def down_grad_kernel(hid_ref, d_ffn_ref, core_ref, *outs):
    total = tn(hid_ref[...], d_ffn_ref[...])
    if len(outs) == 1:
        outs[0][...] = total.astype(BF16)
    else:
        shared_out(core_ref, total, outs, outs[0].shape[1])


def down_grad(hid, d_ffn, core, bits):
    rows = FF >> len(bits)
    shape, spec = (FF, D), pl.BlockSpec((CHUNK, D), lambda j: (j, 0))
    outs = 1
    if rows % 16 == 0:
        outs, shape = 2, (FF // (2 * rows), rows, D)
        spec = pl.BlockSpec((CHUNK // (2 * rows), rows, D), lambda j: (j, 0, 0))
    got = pl.pallas_call(
        down_grad_kernel,
        grid=(FF // CHUNK,),
        in_specs=[
            pl.BlockSpec((ROWS, CHUNK), lambda j: (0, j)),
            pl.BlockSpec((ROWS, D), lambda j: (0, 0)),
            pl.BlockSpec(memory_space=pltpu.SMEM),
        ],
        out_specs=[spec] * outs,
        out_shape=[jax.ShapeDtypeStruct(shape, BF16)] * outs,
        compiler_params=pltpu.CompilerParams(vmem_limit_bytes=VMEM_LIMIT),
        name="down_grad",
    )(hid, d_ffn, core)
    if outs == 1:
        return split_cores(got[0], bits)
    return [a.reshape(2, -1, rows, D) for a in got]


def feed_back_kernel(
    h1_ref, n2_ref, diff_ref, cols_ref, gain_ref, router_ref, g_ref, u_ref, d_ffn_ref,
    wg_ref, wu_ref, wd_ref, core_ref,
    *rest,
):
    *grads, da_ref, part_ref, sums_ref, d_gate, d_up = rest
    step = pl.program_id(0)

    @pl.when(step == 0)
    def _():
        part_ref[...] = jnp.zeros_like(part_ref)

    for start in range(0, SLAB, CHUNK):
        span = slice(start, start + CHUNK)
        d_hidden = nt(d_ffn_ref[...], rows_of(wd_ref, start, CHUNK))
        gate = g_ref[:, span].astype(F32)
        up = u_ref[:, span].astype(F32)
        sig = jax.nn.sigmoid(gate)
        d_gate[:, span] = (d_hidden * up * sig * (1.0 + gate * (1.0 - sig))).astype(BF16)
        d_up[:, span] = (d_hidden * gate * sig).astype(BF16)
        for half, source in enumerate((d_gate, d_up)):
            total = tn(source[:, span], n2_ref[...])
            if len(grads) == 1:
                grads[0][half, span] = total.astype(BF16)
            else:
                rows = grads[0].shape[2]
                spots = slice(start // (2 * rows), (start + CHUNK) // (2 * rows))
                shared_out(core_ref, total, [a.at[half, spots] for a in grads], rows)
    part_ref[...] += nn(d_gate[...], rows_of(wg_ref)) + nn(d_up[...], rows_of(wu_ref))

    @pl.when(step == pl.num_programs(0) - 1)
    def _():
        h1 = h1_ref[...]
        inv = lax.rsqrt(jnp.mean(h1 * h1, axis=-1, keepdims=True) + EPS)
        d_norm = part_ref[...]
        sums_ref[...] = jnp.broadcast_to(
            jnp.sum(d_norm * h1 * inv, axis=0, keepdims=True), sums_ref.shape
        )
        scaled = d_norm * gain_ref[...]
        d_inner = inv * scaled - h1 * inv**3 * jnp.mean(scaled * h1, axis=-1, keepdims=True)
        diff = diff_ref[...]
        da_ref[...] = (cols_ref[:, 0:1] * diff + d_inner).astype(BF16)
        part_ref[...] = diff + cols_ref[:, 1:2] * router_ref[...] + d_inner


def feed_back(h1, n2, diff, cols, gain, router, g, u, d_ffn, packs, core, bits):
    rows = 2 * FF >> len(bits)
    spec, outs, shape = pl.BlockSpec((2, SLAB, D), lambda j: (0, j, 0)), 1, (2, FF, D)
    if rows % 16 == 0:
        outs, shape = 2, (2, FF // (2 * rows), rows, D)
        spec = pl.BlockSpec((2, SLAB // (2 * rows), rows, D), lambda j: (0, j, 0, 0))
    whole = lambda *shape: pl.BlockSpec(shape, lambda j: (0,) * len(shape))
    fixed = lambda *shape: pl.BlockSpec(
        shape, lambda j: (0,) * len(shape), pipeline_mode=pl.Buffered(1)
    )
    *grads, da, part, sums = pl.pallas_call(
        feed_back_kernel,
        grid=(FF // SLAB,),
        in_specs=[
            fixed(ROWS, D),
            fixed(ROWS, D),
            fixed(ROWS, D),
            fixed(ROWS, 128),
            fixed(1, D),
            fixed(1, D),
            pl.BlockSpec((ROWS, SLAB), lambda j: (0, j)),
            pl.BlockSpec((ROWS, SLAB), lambda j: (0, j)),
            fixed(ROWS, D),
            *feed_specs(packs),
            pl.BlockSpec(memory_space=pltpu.SMEM),
        ],
        out_specs=[
            *[spec] * outs,
            whole(ROWS, D),
            whole(ROWS, D),
            whole(8, D),
        ],
        out_shape=[
            *[jax.ShapeDtypeStruct(shape, BF16)] * outs,
            jax.ShapeDtypeStruct((ROWS, D), BF16),
            jax.ShapeDtypeStruct((ROWS, D), F32),
            jax.ShapeDtypeStruct((8, D), F32),
        ],
        scratch_shapes=[
            pltpu.VMEM((ROWS, SLAB), BF16),
            pltpu.VMEM((ROWS, SLAB), BF16),
        ],
        compiler_params=pltpu.CompilerParams(vmem_limit_bytes=VMEM_LIMIT),
        name="feed_back",
    )(h1, n2, diff, cols, gain, router, g, u, d_ffn, *packs, core)
    if outs == 1:
        grads = split_cores(grads[0].reshape(2 * FF, D), bits)
    return [*grads, da, part, sums]


def attend_back_kernel(
    first, final, da_ref, part_ref, x_ref, n1_ref, gain_ref, cos_ref, sin_ref, aux_ref, row_ref,
    q_ref, k_ref, v_ref, o_ref, l_ref, wq_ref, wk_ref, wv_ref, wo0_ref, wo1_ref, wo2_ref,
    *rest,
):
    pack_ref, dn1, grad_ref, sums_ref, bias, wide_q, wide_do, dq, stage, sems = rest[-10:]
    group = pl.program_id(0)
    per = D // KV_HEADS

    @pl.when(group == 0)
    def _():
        bias[...] = jnp.where(aux_ref[:, 3:4] <= row_ref[0:1, :], 0.0, NEG)
        wide_q[...] = jnp.zeros_like(wide_q)
        wide_do[...] = jnp.zeros_like(wide_do)
        dn1[...] = rest[0][...] if len(rest) > 10 else jnp.zeros_like(dn1)

    w_out = jnp.concatenate([wo0_ref[...], wo1_ref[...], wo2_ref[...]], axis=0)
    d_heads = nt(da_ref[...], w_out)
    d_low = d_heads.astype(BF16)
    stage[per + 2 * HEAD :] = tn(o_ref[0], da_ref[...]).astype(BF16)
    copies, top = [], 0
    for rows, base in ((per, 0), (HEAD, D), (HEAD, D + KV_WIDTH), (per, QKV_COLS)):
        place = pl.multiple_of(base + (first + group) * rows, HEAD)
        copies.append(
            pltpu.make_async_copy(
                stage.at[top : top + rows], pack_ref.at[pl.ds(place, rows)], sems.at[len(copies)]
            )
        )
        top += rows
    copies[3].start()
    both = d_low.astype(F32) * o_ref[0].astype(F32)
    key, value = k_ref[0], v_ref[0]
    d_key = jnp.zeros((ROWS, HEAD), F32)
    d_value = jnp.zeros((ROWS, HEAD), F32)
    d_queries = []
    ones = jnp.ones((8, HEAD), F32)
    for head in range(PER_KV):
        span = slice(head * HEAD, (head + 1) * HEAD)
        wide_q[:ROWS] = q_ref[head]
        wide_do[:ROWS] = d_low[:, span]
        inside = lax.dot_general(
            ones, both[:, span], (((1,), (1,)), ((), ())),
            preferred_element_type=F32, precision=lax.Precision.HIGHEST,
        )
        inside = jnp.concatenate([inside, jnp.zeros((8, WIDE - ROWS), F32)], axis=1)
        for start, stop, reach in TILES:
            end = start + TILE
            reach = min(reach, ROWS)
            scores = nt(key[:reach], wide_q[start:end]) * 0.125 + bias[:reach, start:end]
            probs = jnp.exp(scores - l_ref[0, head : head + 1, start:end])
            d_probs = nt(value[:reach], wide_do[start:end])
            d_scores = (probs * (d_probs - inside[0:1, start:end])).astype(BF16)
            add_k = nn(d_scores, wide_q[start:end])
            add_v = nn(probs.astype(BF16), wide_do[start:end])
            if reach < ROWS:
                rest = jnp.zeros((ROWS - reach, HEAD), F32)
                add_k = jnp.concatenate([add_k, rest], axis=0)
                add_v = jnp.concatenate([add_v, rest], axis=0)
            d_key += add_k
            d_value += add_v
            dq[start:end] = tn(d_scores, key[:reach]) * 0.125
        d_queries.append(dq[:ROWS])
    turned_back = turned(
        jnp.concatenate(d_queries + [d_key * 0.125], axis=1), cos_ref[...], -sin_ref[...]
    )
    d_mixed = jnp.concatenate(turned_back + [d_value], axis=1).astype(BF16)
    stage[: per + 2 * HEAD] = tn(d_mixed, n1_ref[...]).astype(BF16)
    for copy in copies[:3]:
        copy.start()
    packed = jnp.concatenate([wq_ref[...], wk_ref[...], wv_ref[...]], axis=0)
    dn1[...] += nn(d_mixed, packed)
    for copy in copies:
        copy.wait()

    if not final:
        return

    @pl.when(group == pl.num_programs(0) - 1)
    def _():
        x = x_ref[...].astype(F32)
        inv = lax.rsqrt(jnp.mean(x * x, axis=-1, keepdims=True) + EPS)
        d_norm = dn1[...]
        sums_ref[...] = jnp.broadcast_to(
            jnp.sum(d_norm * x * inv, axis=0, keepdims=True), sums_ref.shape
        )
        scaled = d_norm * gain_ref[...]
        d_x = inv * scaled - x * inv**3 * jnp.mean(scaled * x, axis=-1, keepdims=True)
        grad_ref[...] = (part_ref[...] + d_x).astype(BF16)


def attend_back(first, count, given, so_far):
    whole = lambda *shape: pl.BlockSpec(shape, lambda g: (0,) * len(shape))
    fixed = lambda *shape: pl.BlockSpec(
        shape, lambda g: (0,) * len(shape), pipeline_mode=pl.Buffered(1)
    )
    per = D // KV_HEADS
    final = first + count == KV_HEADS
    kept = pl.BlockSpec(memory_space=pl.ANY)
    return pl.pallas_call(
        functools.partial(attend_back_kernel, first, final),
        grid=(count,),
        in_specs=[
            fixed(ROWS, D),
            fixed(ROWS, D),
            fixed(ROWS, D),
            fixed(ROWS, D),
            fixed(1, D),
            fixed(ROWS, HEAD),
            fixed(ROWS, HEAD),
            fixed(ROWS, 8),
            fixed(8, WIDE),
            pl.BlockSpec((PER_KV, ROWS, HEAD), lambda g: (first + g, 0, 0)),
            pl.BlockSpec((1, ROWS, HEAD), lambda g: (first + g, 0, 0)),
            pl.BlockSpec((1, ROWS, HEAD), lambda g: (first + g, 0, 0)),
            pl.BlockSpec((1, ROWS, per), lambda g: (first + g, 0, 0)),
            pl.BlockSpec((1, 8, WIDE), lambda g: (first + g, 0, 0)),
            *weight_specs(first),
            *([fixed(ROWS, D), kept] if so_far else []),
        ],
        out_specs=[
            kept,
            whole(ROWS, D),
            whole(ROWS, D),
            whole(8, D),
        ],
        out_shape=[
            jax.ShapeDtypeStruct((QKV_COLS + D, D), BF16),
            jax.ShapeDtypeStruct((ROWS, D), F32),
            jax.ShapeDtypeStruct((ROWS, D), BF16),
            jax.ShapeDtypeStruct((8, D), F32),
        ],
        scratch_shapes=[
            pltpu.VMEM((ROWS, WIDE), F32),
            pltpu.VMEM((WIDE, HEAD), BF16),
            pltpu.VMEM((WIDE, HEAD), BF16),
            pltpu.VMEM((WIDE, HEAD), F32),
            pltpu.VMEM((2 * (per + HEAD), D), BF16),
            pltpu.SemaphoreType.DMA((4,)),
        ],
        input_output_aliases={21: 0} if so_far else {},
        compiler_params=pltpu.CompilerParams(vmem_limit_bytes=VMEM_LIMIT),
        name="attend_back",
    )(*given, *so_far)


def on_device(states, teacher, validity, chosen, attn_pack, gate_up, down_proj, norm_gains, router):
    seq_count, block_rows, width = states.shape
    ctx_count = lax.axis_size("ctx")
    if seq_count != ctx_count:
        raise ValueError("seq_count")
    seq_length = block_rows * ctx_count
    bits = device_bits()
    gain_one, gain_two = norm_gains[0:1], norm_gains[1:2]
    core = own_bit(bits[-1]).astype(jnp.int32).reshape(1)

    feed_rows = jnp.concatenate([gate_up.T, down_proj.T], axis=0)
    packs = lax.all_gather(feed_rows, ("dp", "ctx"), axis=0)
    thin = down_proj.shape[1]
    if thin % 16:
        broad = packs[:, : 2 * thin].reshape(2 * FF, width)
        packs = (broad, broad, packs[:, 2 * thin :].reshape(FF, width))
    else:
        packs = (packs,) * 3
    flags = to_sequence((validity + 2 * chosen).reshape(seq_count, 1, block_rows))
    x_seq = to_sequence(states).reshape(seq_length, width)
    attn_in = Gather(attn_pack.T, bits)
    start(attn_in)
    flags = wait([attn_in], flags)
    start(attn_in)
    wait([attn_in])
    start(attn_in)

    flags = flags.reshape(seq_length)
    chosen_seq, valid_seq = flags >> 1, flags & 1
    place = jnp.arange(seq_length)
    rank = jnp.sum(jnp.where(place[:, None] < place[None, :], chosen_seq[:, None], 0), axis=0)
    slot = jnp.where(chosen_seq > 0, rank, -1)
    pick = (jnp.arange(ROWS)[:, None] == slot[None, :]).astype(BF16)
    picked = pick.astype(F32)
    pos = jnp.sum(picked * place.astype(F32)[None, :], axis=1)
    valid = jnp.sum(picked * valid_seq.astype(F32)[None, :], axis=1)
    live = (jnp.arange(ROWS) < jnp.sum(chosen_seq)).astype(F32)
    half = HEAD // 2
    freqs = THETA ** (-(jnp.arange(half).astype(F32) * 2.0 / HEAD))
    angles = pos[:, None] * freqs[None, :]
    cosine, sine = jnp.cos(angles), jnp.sin(angles)
    cosine = jnp.concatenate([cosine, cosine], axis=1)
    sine = jnp.concatenate([-sine, sine], axis=1)
    block = jnp.floor(pos / block_rows)
    key_block = jnp.where(valid * live > 0.5, block, 1e6)
    aux = jnp.stack([valid, live, block, key_block] + [jnp.zeros_like(pos)] * 4, axis=1)
    row = jnp.stack([block, key_block] + [jnp.zeros_like(pos)] * 6, axis=0)
    row = jnp.pad(row, ((0, 0), (0, WIDE - ROWS)), constant_values=1e6)
    router_row = router[None, :]

    x_seq, pick, cosine, sine, aux, row = wait(
        [attn_in], x_seq, pick, cosine, sine, aux, row
    )
    start(attn_in)
    x_low = dot(pick, x_seq, ((1,), (0,))).astype(BF16)
    x_low = wait([attn_in], x_low)
    start(attn_in)
    wait([attn_in])
    finish(attn_in)
    w_attn = attn_in.part
    (late,) = join(teacher, w_attn)[:1]
    t_seq = to_sequence(late).reshape(seq_length, width)

    n1, q, k, v, o, lse, h1 = attend(x_low, gain_one, cosine, sine, aux, row, w_attn)
    t_low = dot(pick, t_seq, ((1,), (0,))).astype(BF16)
    n2, g, u, hid, y, diff, cols, sums, d_ffn = feed(
        h1, x_low, t_low, aux, gain_two, router_row, packs
    )
    energy = jnp.sum(sums[1])

    def spread(compact):
        whole = dot(compact, pick, ((0,), (0,))).astype(BF16)
        return whole.reshape(width, ctx_count, block_rows).transpose(1, 0, 2)

    def to_home(columns):
        return to_sequence(columns.transpose(0, 2, 1))

    down = Scatter(*down_grad(hid, d_ffn, core, bits), bits)
    start(down)
    d_ffn, out_columns = wait([down], d_ffn, spread(y))
    out_home = to_home(out_columns)
    d_ffn = start_ahead([down], d_ffn)
    *grad_gu, da, part, two = feed_back(
        h1, n2, diff, cols, gain_two, router_row, g, u, d_ffn, packs, core, bits
    )
    da, out_home, *grad_gu = wait([down], da, out_home, *grad_gu)
    wide = Scatter(*grad_gu, bits)
    start(wide, down)
    da = wait([wide], da)
    da = start_ahead([wide], da)

    given = (da, part, x_low, n1, gain_one, cosine, sine, aux, row, q, k, v, o, lse)
    given += (w_attn,) * 6
    so_far = []
    for first, count in SPLIT:
        grad_attn, dn1, d_states, one = attend_back(first, count, given, so_far)
        if first + count < KV_HEADS:
            dn1 = wait([wide, down], dn1)
            dn1 = start_ahead([wide, down], dn1)
        so_far = [dn1, grad_attn]
    grad_attn, d_states = wait([wide, down], grad_attn, d_states)
    attn = Scatter(*split_cores(grad_attn, bits), bits, late=True)

    x_home = states.astype(F32)
    still = (chosen == 0)[..., None]
    valid_home = validity.astype(F32)[..., None]
    apart = valid_home * (x_home - teacher.astype(F32))
    energy = energy + 0.5 * jnp.sum(jnp.where(still, apart * apart, 0.0))
    scalars = jnp.concatenate(
        [energy[None], jnp.sum(validity).astype(F32)[None], jnp.zeros((D - 2,), F32)]
    )
    total = Total(jnp.stack([one[0], two[0], sums[0], scalars], axis=0), bits)

    start(attn, wide, down, total)
    columns = wait([attn, total], spread(d_states))
    grad_home = to_home(columns)
    take(wide, down)
    while attn.step < len(bits):
        start(attn, wide, down, total)
        if attn.step < len(bits):
            wait([attn, total])
            take(wide, down)
    grad_home, attn.mine = join(grad_home, attn.mine)
    take(attn, wide, down, total)
    finish(attn, wide, down, total)
    attn_part, gu_part, down_part = attn.part, wide.part, down.part

    states_out = jnp.where(still, states, out_home)
    states_grad = jnp.where(still, apart, grad_home.astype(F32))

    small = total.part
    mse_loss = 2.0 * small[3, 0] / (small[3, 1] * D)
    return (
        states_out,
        mse_loss,
        states_grad,
        attn_part.T,
        gu_part.T,
        down_part.T,
        small[0:2],
        small[2],
    )


def solution(mesh):
    tokens = P("dp", "ctx", None)
    flags = P("dp", "ctx")
    packs = P(None, ("dp", "ctx"))
    return jax.shard_map(
        on_device,
        mesh=mesh,
        in_specs=(tokens, tokens, flags, flags, packs, packs, packs, P(), P()),
        out_specs=(tokens, P(), tokens, packs, packs, packs, P(), P()),
        check_vma=False,
    )
```

```python
import functools

import jax
import jax.numpy as jnp
from jax import lax
from jax.experimental import pallas as pl
from jax.experimental.pallas import tpu as pltpu
from jax.sharding import PartitionSpec as P

D = 960
HEADS = 15
KV_HEADS = 5
HEAD = 64
FF = 2560
CHOSEN = 640
PER_KV = HEADS // KV_HEADS
KV_WIDTH = KV_HEADS * HEAD
QKV_COLS = D + 2 * KV_WIDTH
ROWS = 656
TILE = 256
WIDE = 768
SLAB = 1280
SPLIT = ((0, 3), (3, 2))
CHUNK = 640
TILES = ((0, 256, 512), (256, 512, 768), (512, ROWS, 768))
NEG = -1e30
VMEM_LIMIT = 62 * 1024 * 1024

EPS = 1e-05
THETA = 10000.0
F32 = jnp.float32
BF16 = jnp.bfloat16


def device_bits():
    found = []
    for name in ("dp", "ctx"):
        count = lax.axis_size(name)
        found += [(name, bit) for bit in reversed(range(count.bit_length() - 1))]
    return found


def swap(value, place):
    name, bit = place
    pairs = [(i, i ^ (1 << bit)) for i in range(lax.axis_size(name))]
    return lax.ppermute(value, name, pairs)


def own_bit(place):
    name, bit = place
    return (lax.axis_index(name) >> bit) & 1


def routes(bits):
    count = len(bits)
    far = list(range(1, count - 3))
    return [far + [count - 3, count - 2, count - 1], far + [count - 2, count - 3, count - 1]]


def late_routes(bits):
    count = len(bits)
    far = list(range(count - 4, 0, -1))
    return [[count - 3] + far + [count - 2], far + [count - 3, count - 2]]


def join(*values):
    return lax.optimization_barrier(values)


def own_bits(bits):
    return jnp.stack([own_bit(place) for place in bits]).astype(jnp.int32)


def order_kernel(spots, own, mine0, other0, mine1, other1, out, sems):
    last = len(spots[0])

    def copies(place):
        found = []
        for half, (mine, other) in enumerate(((mine0, other0), (mine1, other1))):
            slot = 0
            for level, spot in enumerate(spots[half]):
                slot = slot + ((((place >> level) & 1) ^ own[spot]) << (last - spot))
            core = own[last + 1]
            for k, (source, side) in enumerate(((mine, core), (other, 1 - core))):
                found.append(
                    pltpu.make_async_copy(
                        source.at[place], out.at[half, slot, side], sems.at[2 * half + k, place]
                    )
                )
        return found

    def begin(place, carry):
        for copy in copies(place):
            copy.start()
        return carry

    def end(place, carry):
        for copy in copies(place):
            copy.wait()
        return carry

    count = mine0.shape[0]
    lax.fori_loop(0, count, begin, 0)
    lax.fori_loop(0, count, end, 0)


class Gather:
    def __init__(self, shard, bits):
        self.bits = bits
        self.halves, self.routes = [shard[None]], routes(bits)
        self.step, self.part = 0, None
        self.got = []

    def send(self):
        if self.step == 0:
            self.got = [swap(self.halves[0], self.bits[0])]
        else:
            spots = [route[self.step - 1] for route in self.routes]
            self.got = [swap(h, self.bits[s]) for h, s in zip(self.halves, spots)]
        self.step += 1

    def take(self):
        if self.step == 1:
            low_side = own_bit(self.bits[0]) == 0
            shard, other = self.halves[0], self.got[0]
            self.halves = [jnp.where(low_side, shard, other), jnp.where(low_side, other, shard)]
        elif self.step < len(self.bits):
            self.halves = [jnp.concatenate(p, axis=0) for p in zip(self.halves, self.got)]
        else:
            self.part = self.ordered()

    def ordered(self):
        count, rows, width = self.halves[0].shape
        anywhere = pl.BlockSpec(memory_space=pl.ANY)
        out = pl.pallas_call(
            functools.partial(order_kernel, [r[:-1] for r in self.routes]),
            in_specs=[pl.BlockSpec(memory_space=pltpu.SMEM)] + [anywhere] * 4,
            out_specs=pl.BlockSpec(memory_space=pltpu.VMEM),
            out_shape=jax.ShapeDtypeStruct((2, count, 2, rows, width), BF16),
            scratch_shapes=[pltpu.SemaphoreType.DMA((4, count))],
            compiler_params=pltpu.CompilerParams(vmem_limit_bytes=VMEM_LIMIT),
            name="order",
        )(own_bits(self.bits), self.halves[0], self.got[0], self.halves[1], self.got[1])
        return out.reshape(-1, width)


class Scatter:
    def __init__(self, keep, send, bits, late=False):
        self.bits = bits
        self.keep, self.out = keep, send
        self.routes = late_routes(bits) if late else [route[-2::-1] for route in routes(bits)]
        self.step, self.part = 0, None
        self.got, self.outs = [], []

    def choose(self, half, choice):
        total = 0.0
        for array, held in self.parts[half]:
            rows, width = array.shape[-2:]
            run = [h for h in held if h in choice]
            if run:
                at, index = held.index(run[0]), 0
                for spot in run:
                    index = 2 * index + choice[spot]
                cube = array.reshape(1 << at, 1 << len(run), -1, width)
                array = lax.dynamic_index_in_dim(cube, index, 1, keepdims=False)
            total = total + array.reshape(-1, rows, width).astype(F32)
        return total

    def cut(self):
        last = len(self.bits) - 1
        if self.step == 0:
            self.outs, self.spots = [self.out], [last]
        elif self.step < last:
            self.outs, self.spots = [], []
            for half, route in enumerate(self.routes):
                choice = {s: own_bit(self.bits[s]) for s in route[: self.step]}
                spot = route[self.step - 1]
                choice[spot] = 1 - choice[spot]
                self.outs.append(self.choose(half, choice).astype(BF16))
                self.spots.append(spot)
        else:
            low_side = own_bit(self.bits[0]) == 0
            sums = []
            for half, route in enumerate(self.routes):
                sums.append(self.choose(half, {s: own_bit(self.bits[s]) for s in route})[0])
            self.mine = jnp.where(low_side, sums[0], sums[1])
            self.outs = [jnp.where(low_side, sums[1], sums[0]).astype(BF16)]
            self.spots = [0]

    def send(self):
        if not self.outs:
            self.cut()
        self.got = [swap(out, self.bits[spot]) for out, spot in zip(self.outs, self.spots)]
        self.outs = []
        self.step += 1

    def take(self):
        if self.step == 1:
            held = sorted(self.routes[0])
            self.parts = [
                [(self.keep[half], held), (self.got[0][half], held)] for half in range(2)
            ]
        elif self.step <= len(self.bits) - 1:
            for parts, got, route in zip(self.parts, self.got, self.routes):
                parts.append((got, sorted(route[self.step - 1 :])))
        else:
            self.part = self.mine + self.got[0].astype(F32)


def split_cores(whole, bits):
    count = 1 << (len(bits) - 2)
    cube = whole.reshape(2 * count, 2, -1, whole.shape[-1])
    mine = own_bit(bits[-1])
    both = [lax.dynamic_index_in_dim(cube, side, 1, keepdims=False) for side in (mine, 1 - mine)]
    return [b.reshape(2, count, -1, whole.shape[-1]) for b in both]


def start(*moves):
    for m in moves:
        if m.part is None and not m.got:
            m.send()


def start_ahead(moves, *values):
    moves = [m for m in moves if m.part is None and not m.got]
    for m in moves:
        m.cut()
    flat = list(join(*values, *[o for m in moves for o in m.outs]))
    values, flat = flat[: len(values)], flat[len(values) :]
    for m in moves:
        m.outs, flat = flat[: len(m.outs)], flat[len(m.outs) :]
        m.send()
    return values if len(values) != 1 else values[0]


def take(*moves):
    for m in moves:
        if m.got:
            m.take()
            m.got = []


def wait(moves, *values):
    moves = [m for m in moves if m.got]
    flat = list(join(*values, *[g for m in moves for g in m.got]))
    values, flat = flat[: len(values)], flat[len(values) :]
    for m in moves:
        m.got, flat = flat[: len(m.got)], flat[len(m.got) :]
    take(*moves)
    return values if len(values) != 1 else values[0]


def finish(*moves):
    while any(m.part is None for m in moves):
        start(*moves)
        take(*moves)


class Total:
    def __init__(self, value, bits):
        self.value, self.bits = value, bits
        self.step, self.part, self.got = 0, None, []

    def send(self):
        self.got = [swap(self.value, self.bits[self.step])]
        self.step += 1

    def take(self):
        self.value = self.value + self.got[0]
        if self.step == len(self.bits):
            self.part = self.value


def dot(left, right, contract):
    return lax.dot_general(left, right, (contract, ((), ())), preferred_element_type=F32)


def to_sequence(blocks):
    return lax.all_to_all(blocks, "ctx", split_axis=0, concat_axis=0, tiled=True)


def nt(left, right):
    return lax.dot_general(left, right, (((1,), (1,)), ((), ())), preferred_element_type=F32)


def nn(left, right):
    return lax.dot_general(left, right, (((1,), (0,)), ((), ())), preferred_element_type=F32)


def tn(left, right):
    return lax.dot_general(left, right, (((0,), (0,)), ((), ())), preferred_element_type=F32)


def turned(values, cosine, sine):
    half = HEAD // 2
    pieces = []
    for start in range(0, values.shape[1], HEAD):
        head = values[:, start : start + HEAD]
        swapped = jnp.concatenate([head[:, half:], head[:, :half]], axis=1)
        pieces.append(head * cosine + swapped * sine)
    return pieces


def weight_specs(first):
    places = [HEADS, HEADS + KV_HEADS] + [QKV_COLS // HEAD + r for r in range(PER_KV)]
    steps = [1, 1] + [PER_KV] * PER_KV
    return [pl.BlockSpec((D // KV_HEADS, D), lambda g: (first + g, 0))] + [
        pl.BlockSpec((HEAD, D), lambda g, p=p, s=s: (p + s * (first + g), 0))
        for p, s in zip(places, steps)
    ]


def attend_kernel(
    x_ref, gain_ref, cos_ref, sin_ref, aux_ref, row_ref, wq_ref, wk_ref, wv_ref, wo0_ref, wo1_ref, wo2_ref,
    n1_ref, q_ref, k_ref, v_ref, o_ref, l_ref, h1_ref,
    bias, keys, vals, lse,
):
    group = pl.program_id(0)

    @pl.when(group == 0)
    def _():
        x = x_ref[...].astype(F32)
        inv = lax.rsqrt(jnp.mean(x * x, axis=-1, keepdims=True) + EPS)
        n1_ref[...] = (x * inv * gain_ref[...]).astype(BF16)
        h1_ref[...] = x
        bias[...] = jnp.where(row_ref[1:2, :] <= aux_ref[:, 2:3], 0.0, NEG)
        keys[...] = jnp.zeros_like(keys)
        vals[...] = jnp.zeros_like(vals)
        lse[...] = jnp.zeros_like(lse)

    packed = jnp.concatenate([wq_ref[...], wk_ref[...], wv_ref[...]], axis=0)
    mixed = nt(n1_ref[...], packed)
    rotated = turned(mixed[:, : D // KV_HEADS + HEAD], cos_ref[...], sin_ref[...])
    key = rotated[PER_KV].astype(BF16)
    value = mixed[:, D // KV_HEADS + HEAD :].astype(BF16)
    k_ref[0] = key
    v_ref[0] = value
    keys[:ROWS] = key
    vals[:ROWS] = value
    for head in range(PER_KV):
        q_ref[head] = rotated[head].astype(BF16)
    lanes = lax.broadcasted_iota(jnp.int32, (1, 128), 1)
    for start, stop, reach in TILES:
        outs = []
        logs = jnp.zeros((stop - start, 128), F32)
        for head in range(PER_KV):
            scores = nt(q_ref[head, start:stop], keys[:reach]) * 0.125 + bias[start:stop, :reach]
            top = jnp.max(scores, axis=-1, keepdims=True)
            expd = jnp.exp(scores - top)
            total = jnp.sum(expd, axis=-1, keepdims=True)
            outs.append(nn(expd.astype(BF16), vals[:reach]) / total)
            logs = jnp.where(lanes == head, top + jnp.log(total), logs)
        o_ref[0, start:stop] = jnp.concatenate(outs, axis=1).astype(BF16)
        lse[start:stop] = logs
    l_ref[0] = lse[...].T[:8]
    h1_ref[...] += nn(o_ref[0], jnp.concatenate([wo0_ref[...], wo1_ref[...], wo2_ref[...]], axis=0))


def attend(x, gain, cosine, sine, aux, row, w_attn):
    whole = lambda *shape: pl.BlockSpec(shape, lambda g: (0,) * len(shape))
    fixed = lambda *shape: pl.BlockSpec(
        shape, lambda g: (0,) * len(shape), pipeline_mode=pl.Buffered(1)
    )
    per = D // KV_HEADS
    return pl.pallas_call(
        attend_kernel,
        grid=(KV_HEADS,),
        in_specs=[
            fixed(ROWS, D),
            fixed(1, D),
            fixed(ROWS, HEAD),
            fixed(ROWS, HEAD),
            fixed(ROWS, 8),
            fixed(8, WIDE),
            *weight_specs(0),
        ],
        out_specs=[
            whole(ROWS, D),
            pl.BlockSpec((PER_KV, ROWS, HEAD), lambda g: (g, 0, 0)),
            pl.BlockSpec((1, ROWS, HEAD), lambda g: (g, 0, 0)),
            pl.BlockSpec((1, ROWS, HEAD), lambda g: (g, 0, 0)),
            pl.BlockSpec((1, ROWS, per), lambda g: (g, 0, 0)),
            pl.BlockSpec((1, 8, WIDE), lambda g: (g, 0, 0)),
            whole(ROWS, D),
        ],
        out_shape=[
            jax.ShapeDtypeStruct((ROWS, D), BF16),
            jax.ShapeDtypeStruct((HEADS, ROWS, HEAD), BF16),
            jax.ShapeDtypeStruct((KV_HEADS, ROWS, HEAD), BF16),
            jax.ShapeDtypeStruct((KV_HEADS, ROWS, HEAD), BF16),
            jax.ShapeDtypeStruct((KV_HEADS, ROWS, per), BF16),
            jax.ShapeDtypeStruct((KV_HEADS, 8, WIDE), F32),
            jax.ShapeDtypeStruct((ROWS, D), F32),
        ],
        scratch_shapes=[
            pltpu.VMEM((ROWS, WIDE), F32),
            pltpu.VMEM((WIDE, HEAD), BF16),
            pltpu.VMEM((WIDE, HEAD), BF16),
            pltpu.VMEM((WIDE, 128), F32),
        ],
        compiler_params=pltpu.CompilerParams(vmem_limit_bytes=VMEM_LIMIT),
        name="attend",
    )(x, gain, cosine, sine, aux, row, *[w_attn] * 6)


def feed_specs(packs):
    if packs[0].ndim == 2:
        return [
            pl.BlockSpec((SLAB, D), lambda j: (j, 0)),
            pl.BlockSpec((SLAB, D), lambda j: (FF // SLAB + j, 0)),
            pl.BlockSpec((SLAB, D), lambda j: (j, 0)),
        ]
    count, rows, _ = packs[0].shape
    thin = rows // 3
    return [
        pl.BlockSpec((SLAB // (2 * thin), 2 * thin, D), lambda j: (j, 0, 0)),
        pl.BlockSpec((SLAB // (2 * thin), 2 * thin, D), lambda j: (FF // SLAB + j, 0, 0)),
        pl.BlockSpec((SLAB // thin, thin, D), lambda j: (j, 2, 0)),
    ]


def rows_of(ref, start=0, size=SLAB):
    if len(ref.shape) == 2:
        return ref[start : start + size]
    each = ref.shape[1]
    return ref[start // each : (start + size) // each].reshape(size, D)


def spread(compact, pick_ref, out_ref):
    size = out_ref.shape[2]
    for block in range(out_ref.shape[0]):
        places = pick_ref[:, block * size : (block + 1) * size]
        out_ref[block] = tn(compact, places).astype(BF16)


def feed_kernel(
    h1_ref, x_ref, t_ref, aux_ref, gain_ref, router_ref, pick_ref, wg_ref, wu_ref, wd_ref,
    n2_ref, g_ref, u_ref, hid_ref, out_ref, diff_ref, cols_ref, sums_ref, d_ffn_ref,
):
    step = pl.program_id(0)

    @pl.when(step == 0)
    def _():
        h1 = h1_ref[...]
        inv = lax.rsqrt(jnp.mean(h1 * h1, axis=-1, keepdims=True) + EPS)
        n2_ref[...] = (h1 * inv * gain_ref[...]).astype(BF16)
        diff_ref[...] = h1 - x_ref[...].astype(F32)

    for start in range(0, SLAB, CHUNK):
        span = slice(start, start + CHUNK)
        gate = nt(n2_ref[...], rows_of(wg_ref, start, CHUNK))
        up = nt(n2_ref[...], rows_of(wu_ref, start, CHUNK))
        g_ref[:, span] = gate.astype(BF16)
        u_ref[:, span] = up.astype(BF16)
        hid_ref[:, span] = (gate * jax.nn.sigmoid(gate) * up).astype(BF16)
    diff_ref[...] += nn(hid_ref[...], rows_of(wd_ref))

    @pl.when(step == pl.num_programs(0) - 1)
    def _():
        x = x_ref[...].astype(F32)
        branch = diff_ref[...]
        valid, live = aux_ref[:, 0:1], aux_ref[:, 1:2]
        prob = jax.nn.sigmoid(jnp.sum(x * router_ref[...], axis=-1, keepdims=True))
        mix = live * prob
        result = x + mix * branch
        spread(result.astype(BF16), pick_ref, out_ref)
        diff = valid * (result - t_ref[...].astype(F32))
        d_logit = live * jnp.sum(diff * branch, axis=-1, keepdims=True) * prob * (1.0 - prob)
        diff_ref[...] = diff
        d_ffn_ref[...] = (mix * diff).astype(BF16)
        lanes = lax.broadcasted_iota(jnp.int32, (1, 128), 1)
        cols_ref[...] = jnp.where(lanes == 0, mix, jnp.where(lanes == 1, d_logit, 0.0))
        sums_ref[...] = jnp.concatenate(
            [
                jnp.sum(d_logit * x, axis=0, keepdims=True),
                0.5 * jnp.sum(diff * diff, axis=0, keepdims=True),
                jnp.zeros((6, D), F32),
            ],
            axis=0,
        )


def feed(h1, x, t, aux, gain, router, pick, packs, blocks):
    whole = lambda *shape: pl.BlockSpec(shape, lambda j: (0,) * len(shape))
    fixed = lambda *shape: pl.BlockSpec(
        shape, lambda j: (0,) * len(shape), pipeline_mode=pl.Buffered(1)
    )
    return pl.pallas_call(
        feed_kernel,
        grid=(FF // SLAB,),
        in_specs=[
            fixed(ROWS, D),
            fixed(ROWS, D),
            fixed(ROWS, D),
            fixed(ROWS, 8),
            fixed(1, D),
            fixed(1, D),
            fixed(*pick.shape),
            *feed_specs(packs),
        ],
        out_specs=[
            whole(ROWS, D),
            pl.BlockSpec((ROWS, SLAB), lambda j: (0, j)),
            pl.BlockSpec((ROWS, SLAB), lambda j: (0, j)),
            pl.BlockSpec((ROWS, SLAB), lambda j: (0, j)),
            whole(*blocks),
            whole(ROWS, D),
            whole(ROWS, 128),
            whole(8, D),
            whole(ROWS, D),
        ],
        out_shape=[
            jax.ShapeDtypeStruct((ROWS, D), BF16),
            jax.ShapeDtypeStruct((ROWS, FF), BF16),
            jax.ShapeDtypeStruct((ROWS, FF), BF16),
            jax.ShapeDtypeStruct((ROWS, FF), BF16),
            jax.ShapeDtypeStruct(blocks, BF16),
            jax.ShapeDtypeStruct((ROWS, D), F32),
            jax.ShapeDtypeStruct((ROWS, 128), F32),
            jax.ShapeDtypeStruct((8, D), F32),
            jax.ShapeDtypeStruct((ROWS, D), BF16),
        ],
        compiler_params=pltpu.CompilerParams(vmem_limit_bytes=VMEM_LIMIT),
        name="feed",
    )(h1, x, t, aux, gain, router, pick, *packs)


def shared_out(core_ref, total, refs, rows):
    low = core_ref[0] == 0
    for pair in range(total.shape[0] // (2 * rows)):
        even = total[2 * pair * rows : (2 * pair + 1) * rows]
        odd = total[(2 * pair + 1) * rows : (2 * pair + 2) * rows]
        refs[0][pair] = jnp.where(low, even, odd).astype(BF16)
        refs[1][pair] = jnp.where(low, odd, even).astype(BF16)


def down_grad_kernel(hid_ref, d_ffn_ref, core_ref, *outs):
    total = tn(hid_ref[...], d_ffn_ref[...])
    if len(outs) == 1:
        outs[0][...] = total.astype(BF16)
    else:
        shared_out(core_ref, total, outs, outs[0].shape[1])


def down_grad(hid, d_ffn, core, bits):
    rows = FF >> len(bits)
    shape, spec = (FF, D), pl.BlockSpec((CHUNK, D), lambda j: (j, 0))
    outs = 1
    if rows % 16 == 0:
        outs, shape = 2, (FF // (2 * rows), rows, D)
        spec = pl.BlockSpec((CHUNK // (2 * rows), rows, D), lambda j: (j, 0, 0))
    got = pl.pallas_call(
        down_grad_kernel,
        grid=(FF // CHUNK,),
        in_specs=[
            pl.BlockSpec((ROWS, CHUNK), lambda j: (0, j)),
            pl.BlockSpec((ROWS, D), lambda j: (0, 0)),
            pl.BlockSpec(memory_space=pltpu.SMEM),
        ],
        out_specs=[spec] * outs,
        out_shape=[jax.ShapeDtypeStruct(shape, BF16)] * outs,
        compiler_params=pltpu.CompilerParams(vmem_limit_bytes=VMEM_LIMIT),
        name="down_grad",
    )(hid, d_ffn, core)
    if outs == 1:
        return split_cores(got[0], bits)
    return [a.reshape(2, -1, rows, D) for a in got]


def feed_back_kernel(
    h1_ref, n2_ref, diff_ref, cols_ref, gain_ref, router_ref, g_ref, u_ref, d_ffn_ref,
    wg_ref, wu_ref, wd_ref, core_ref,
    *rest,
):
    *grads, da_ref, part_ref, sums_ref, d_gate, d_up = rest
    step = pl.program_id(0)

    @pl.when(step == 0)
    def _():
        part_ref[...] = jnp.zeros_like(part_ref)

    for start in range(0, SLAB, CHUNK):
        span = slice(start, start + CHUNK)
        d_hidden = nt(d_ffn_ref[...], rows_of(wd_ref, start, CHUNK))
        gate = g_ref[:, span].astype(F32)
        up = u_ref[:, span].astype(F32)
        sig = jax.nn.sigmoid(gate)
        d_gate[:, span] = (d_hidden * up * sig * (1.0 + gate * (1.0 - sig))).astype(BF16)
        d_up[:, span] = (d_hidden * gate * sig).astype(BF16)
        for half, source in enumerate((d_gate, d_up)):
            total = tn(source[:, span], n2_ref[...])
            if len(grads) == 1:
                grads[0][half, span] = total.astype(BF16)
            else:
                rows = grads[0].shape[2]
                spots = slice(start // (2 * rows), (start + CHUNK) // (2 * rows))
                shared_out(core_ref, total, [a.at[half, spots] for a in grads], rows)
    part_ref[...] += nn(d_gate[...], rows_of(wg_ref)) + nn(d_up[...], rows_of(wu_ref))

    @pl.when(step == pl.num_programs(0) - 1)
    def _():
        h1 = h1_ref[...]
        inv = lax.rsqrt(jnp.mean(h1 * h1, axis=-1, keepdims=True) + EPS)
        d_norm = part_ref[...]
        sums_ref[...] = jnp.broadcast_to(
            jnp.sum(d_norm * h1 * inv, axis=0, keepdims=True), sums_ref.shape
        )
        scaled = d_norm * gain_ref[...]
        d_inner = inv * scaled - h1 * inv**3 * jnp.mean(scaled * h1, axis=-1, keepdims=True)
        diff = diff_ref[...]
        da_ref[...] = (cols_ref[:, 0:1] * diff + d_inner).astype(BF16)
        part_ref[...] = diff + cols_ref[:, 1:2] * router_ref[...] + d_inner


def feed_back(h1, n2, diff, cols, gain, router, g, u, d_ffn, packs, core, bits):
    rows = 2 * FF >> len(bits)
    spec, outs, shape = pl.BlockSpec((2, SLAB, D), lambda j: (0, j, 0)), 1, (2, FF, D)
    if rows % 16 == 0:
        outs, shape = 2, (2, FF // (2 * rows), rows, D)
        spec = pl.BlockSpec((2, SLAB // (2 * rows), rows, D), lambda j: (0, j, 0, 0))
    whole = lambda *shape: pl.BlockSpec(shape, lambda j: (0,) * len(shape))
    fixed = lambda *shape: pl.BlockSpec(
        shape, lambda j: (0,) * len(shape), pipeline_mode=pl.Buffered(1)
    )
    *grads, da, part, sums = pl.pallas_call(
        feed_back_kernel,
        grid=(FF // SLAB,),
        in_specs=[
            fixed(ROWS, D),
            fixed(ROWS, D),
            fixed(ROWS, D),
            fixed(ROWS, 128),
            fixed(1, D),
            fixed(1, D),
            pl.BlockSpec((ROWS, SLAB), lambda j: (0, j)),
            pl.BlockSpec((ROWS, SLAB), lambda j: (0, j)),
            fixed(ROWS, D),
            *feed_specs(packs),
            pl.BlockSpec(memory_space=pltpu.SMEM),
        ],
        out_specs=[
            *[spec] * outs,
            whole(ROWS, D),
            whole(ROWS, D),
            whole(8, D),
        ],
        out_shape=[
            *[jax.ShapeDtypeStruct(shape, BF16)] * outs,
            jax.ShapeDtypeStruct((ROWS, D), BF16),
            jax.ShapeDtypeStruct((ROWS, D), F32),
            jax.ShapeDtypeStruct((8, D), F32),
        ],
        scratch_shapes=[
            pltpu.VMEM((ROWS, SLAB), BF16),
            pltpu.VMEM((ROWS, SLAB), BF16),
        ],
        compiler_params=pltpu.CompilerParams(vmem_limit_bytes=VMEM_LIMIT),
        name="feed_back",
    )(h1, n2, diff, cols, gain, router, g, u, d_ffn, *packs, core)
    if outs == 1:
        grads = split_cores(grads[0].reshape(2 * FF, D), bits)
    return [*grads, da, part, sums]


def attend_back_kernel(
    first, final, da_ref, n1_ref, cos_ref, sin_ref, aux_ref, row_ref,
    q_ref, k_ref, v_ref, o_ref, l_ref, wq_ref, wk_ref, wv_ref, wo0_ref, wo1_ref, wo2_ref,
    *rest,
):
    *rest, bias, wide_q, wide_do, dq, stage, sems = rest
    if final:
        *rest, part_ref, x_ref, gain_ref, pick_ref, pack_ref, dn1, grad_ref, sums_ref = rest
    else:
        *rest, pack_ref, dn1 = rest
    group = pl.program_id(0)
    per = D // KV_HEADS

    @pl.when(group == 0)
    def _():
        bias[...] = jnp.where(aux_ref[:, 3:4] <= row_ref[0:1, :], 0.0, NEG)
        wide_q[...] = jnp.zeros_like(wide_q)
        wide_do[...] = jnp.zeros_like(wide_do)
        dn1[...] = rest[0][...] if rest else jnp.zeros_like(dn1)

    w_out = jnp.concatenate([wo0_ref[...], wo1_ref[...], wo2_ref[...]], axis=0)
    d_heads = nt(da_ref[...], w_out)
    d_low = d_heads.astype(BF16)
    stage[per + 2 * HEAD :] = tn(o_ref[0], da_ref[...]).astype(BF16)
    copies, top = [], 0
    for rows, base in ((per, 0), (HEAD, D), (HEAD, D + KV_WIDTH), (per, QKV_COLS)):
        place = pl.multiple_of(base + (first + group) * rows, HEAD)
        copies.append(
            pltpu.make_async_copy(
                stage.at[top : top + rows], pack_ref.at[pl.ds(place, rows)], sems.at[len(copies)]
            )
        )
        top += rows
    copies[3].start()
    both = d_low.astype(F32) * o_ref[0].astype(F32)
    key, value = k_ref[0], v_ref[0]
    d_key = jnp.zeros((ROWS, HEAD), F32)
    d_value = jnp.zeros((ROWS, HEAD), F32)
    d_queries = []
    ones = jnp.ones((8, HEAD), F32)
    for head in range(PER_KV):
        span = slice(head * HEAD, (head + 1) * HEAD)
        wide_q[:ROWS] = q_ref[head]
        wide_do[:ROWS] = d_low[:, span]
        inside = lax.dot_general(
            ones, both[:, span], (((1,), (1,)), ((), ())),
            preferred_element_type=F32, precision=lax.Precision.HIGHEST,
        )
        inside = jnp.concatenate([inside, jnp.zeros((8, WIDE - ROWS), F32)], axis=1)
        for start, stop, reach in TILES:
            end = start + TILE
            reach = min(reach, ROWS)
            scores = nt(key[:reach], wide_q[start:end]) * 0.125 + bias[:reach, start:end]
            probs = jnp.exp(scores - l_ref[0, head : head + 1, start:end])
            d_probs = nt(value[:reach], wide_do[start:end])
            d_scores = (probs * (d_probs - inside[0:1, start:end])).astype(BF16)
            add_k = nn(d_scores, wide_q[start:end])
            add_v = nn(probs.astype(BF16), wide_do[start:end])
            if reach < ROWS:
                rest = jnp.zeros((ROWS - reach, HEAD), F32)
                add_k = jnp.concatenate([add_k, rest], axis=0)
                add_v = jnp.concatenate([add_v, rest], axis=0)
            d_key += add_k
            d_value += add_v
            dq[start:end] = tn(d_scores, key[:reach]) * 0.125
        d_queries.append(dq[:ROWS])
    turned_back = turned(
        jnp.concatenate(d_queries + [d_key * 0.125], axis=1), cos_ref[...], -sin_ref[...]
    )
    d_mixed = jnp.concatenate(turned_back + [d_value], axis=1).astype(BF16)
    stage[: per + 2 * HEAD] = tn(d_mixed, n1_ref[...]).astype(BF16)
    for copy in copies[:3]:
        copy.start()
    packed = jnp.concatenate([wq_ref[...], wk_ref[...], wv_ref[...]], axis=0)
    dn1[...] += nn(d_mixed, packed)
    for copy in copies:
        copy.wait()

    if not final:
        return

    @pl.when(group == pl.num_programs(0) - 1)
    def _():
        x = x_ref[...].astype(F32)
        inv = lax.rsqrt(jnp.mean(x * x, axis=-1, keepdims=True) + EPS)
        d_norm = dn1[...]
        sums_ref[...] = jnp.broadcast_to(
            jnp.sum(d_norm * x * inv, axis=0, keepdims=True), sums_ref.shape
        )
        scaled = d_norm * gain_ref[...]
        d_x = inv * scaled - x * inv**3 * jnp.mean(scaled * x, axis=-1, keepdims=True)
        spread((part_ref[...] + d_x).astype(BF16), pick_ref, grad_ref)


def attend_back(first, count, given, so_far, closing, blocks):
    whole = lambda *shape: pl.BlockSpec(shape, lambda g: (0,) * len(shape))
    fixed = lambda *shape: pl.BlockSpec(
        shape, lambda g: (0,) * len(shape), pipeline_mode=pl.Buffered(1)
    )
    per = D // KV_HEADS
    final = first + count == KV_HEADS
    kept = pl.BlockSpec(memory_space=pl.ANY)
    return pl.pallas_call(
        functools.partial(attend_back_kernel, first, final),
        grid=(count,),
        in_specs=[
            fixed(ROWS, D),
            fixed(ROWS, D),
            fixed(ROWS, HEAD),
            fixed(ROWS, HEAD),
            fixed(ROWS, 8),
            fixed(8, WIDE),
            pl.BlockSpec((PER_KV, ROWS, HEAD), lambda g: (first + g, 0, 0)),
            pl.BlockSpec((1, ROWS, HEAD), lambda g: (first + g, 0, 0)),
            pl.BlockSpec((1, ROWS, HEAD), lambda g: (first + g, 0, 0)),
            pl.BlockSpec((1, ROWS, per), lambda g: (first + g, 0, 0)),
            pl.BlockSpec((1, 8, WIDE), lambda g: (first + g, 0, 0)),
            *weight_specs(first),
            *([fixed(ROWS, D), kept] if so_far else []),
            *([fixed(*c.shape) for c in closing] if final else []),
        ],
        out_specs=[
            kept,
            whole(ROWS, D),
            *([whole(*blocks), whole(8, D)] if final else []),
        ],
        out_shape=[
            jax.ShapeDtypeStruct((QKV_COLS + D, D), BF16),
            jax.ShapeDtypeStruct((ROWS, D), F32),
            *(
                [jax.ShapeDtypeStruct(blocks, BF16), jax.ShapeDtypeStruct((8, D), F32)]
                if final
                else []
            ),
        ],
        scratch_shapes=[
            pltpu.VMEM((ROWS, WIDE), F32),
            pltpu.VMEM((WIDE, HEAD), BF16),
            pltpu.VMEM((WIDE, HEAD), BF16),
            pltpu.VMEM((WIDE, HEAD), F32),
            pltpu.VMEM((2 * (per + HEAD), D), BF16),
            pltpu.SemaphoreType.DMA((4,)),
        ],
        input_output_aliases={18: 0} if so_far else {},
        compiler_params=pltpu.CompilerParams(vmem_limit_bytes=VMEM_LIMIT),
        name="attend_back",
    )(*given, *so_far, *(closing if final else ()))


def on_device(states, teacher, validity, chosen, attn_pack, gate_up, down_proj, norm_gains, router):
    seq_count, block_rows, width = states.shape
    ctx_count = lax.axis_size("ctx")
    if seq_count != ctx_count:
        raise ValueError("seq_count")
    seq_length = block_rows * ctx_count
    bits = device_bits()
    gain_one, gain_two = norm_gains[0:1], norm_gains[1:2]
    core = own_bit(bits[-1]).astype(jnp.int32).reshape(1)

    feed_rows = jnp.concatenate([gate_up.T, down_proj.T], axis=0)
    packs = lax.all_gather(feed_rows, ("dp", "ctx"), axis=0)
    thin = down_proj.shape[1]
    if thin % 16:
        broad = packs[:, : 2 * thin].reshape(2 * FF, width)
        packs = (broad, broad, packs[:, 2 * thin :].reshape(FF, width))
    else:
        packs = (packs,) * 3
    flags = to_sequence((validity + 2 * chosen).reshape(seq_count, 1, block_rows))
    x_seq = to_sequence(states).reshape(seq_length, width)
    attn_in = Gather(attn_pack.T, bits)
    start(attn_in)
    flags = wait([attn_in], flags)
    start(attn_in)
    wait([attn_in])
    start(attn_in)

    flags = flags.reshape(seq_length)
    chosen_seq, valid_seq = flags >> 1, flags & 1
    place = jnp.arange(seq_length)
    rank = jnp.sum(jnp.where(place[:, None] < place[None, :], chosen_seq[:, None], 0), axis=0)
    slot = jnp.where(chosen_seq > 0, rank, -1)
    pick = (jnp.arange(ROWS)[:, None] == slot[None, :]).astype(BF16)
    picked = pick.astype(F32)
    pos = jnp.sum(picked * place.astype(F32)[None, :], axis=1)
    valid = jnp.sum(picked * valid_seq.astype(F32)[None, :], axis=1)
    live = (jnp.arange(ROWS) < jnp.sum(chosen_seq)).astype(F32)
    half = HEAD // 2
    freqs = THETA ** (-(jnp.arange(half).astype(F32) * 2.0 / HEAD))
    angles = pos[:, None] * freqs[None, :]
    cosine, sine = jnp.cos(angles), jnp.sin(angles)
    cosine = jnp.concatenate([cosine, cosine], axis=1)
    sine = jnp.concatenate([-sine, sine], axis=1)
    block = jnp.floor(pos / block_rows)
    key_block = jnp.where(valid * live > 0.5, block, 1e6)
    aux = jnp.stack([valid, live, block, key_block] + [jnp.zeros_like(pos)] * 4, axis=1)
    row = jnp.stack([block, key_block] + [jnp.zeros_like(pos)] * 6, axis=0)
    row = jnp.pad(row, ((0, 0), (0, WIDE - ROWS)), constant_values=1e6)
    router_row = router[None, :]


    x_home = states.astype(F32)
    still = (chosen == 0)[..., None]
    valid_home = validity.astype(F32)[..., None]
    apart = valid_home * (x_home - teacher.astype(F32))
    energy = 0.5 * jnp.sum(jnp.where(still, apart * apart, 0.0))
    scalars = jnp.concatenate(
        [energy[None], jnp.sum(validity).astype(F32)[None], jnp.zeros((D - 2,), F32)]
    )

    x_seq, pick, cosine, sine, aux, row, scalars = wait(
        [attn_in], x_seq, pick, cosine, sine, aux, row, scalars
    )
    start(attn_in)
    x_low = dot(pick, x_seq, ((1,), (0,))).astype(BF16)
    x_low = wait([attn_in], x_low)
    start(attn_in)
    wait([attn_in])
    finish(attn_in)
    w_attn = attn_in.part
    (late,) = join(teacher, w_attn)[:1]
    t_seq = to_sequence(late).reshape(seq_length, width)

    n1, q, k, v, o, lse, h1 = attend(x_low, gain_one, cosine, sine, aux, row, w_attn)
    t_low = dot(pick, t_seq, ((1,), (0,))).astype(BF16)
    blocks = (ctx_count, width, block_rows)
    n2, g, u, hid, out_columns, diff, cols, sums, d_ffn = feed(
        h1, x_low, t_low, aux, gain_two, router_row, pick, packs, blocks
    )

    def to_home(columns):
        return to_sequence(columns.transpose(0, 2, 1))

    down = Scatter(*down_grad(hid, d_ffn, core, bits), bits)
    start(down)
    d_ffn = wait([down], d_ffn)
    out_home = to_home(out_columns)
    d_ffn = start_ahead([down], d_ffn)
    *grad_gu, da, part, two = feed_back(
        h1, n2, diff, cols, gain_two, router_row, g, u, d_ffn, packs, core, bits
    )
    da, out_home, *grad_gu = wait([down], da, out_home, *grad_gu)
    wide = Scatter(*grad_gu, bits)
    start(wide, down)
    da = wait([wide], da)
    da = start_ahead([wide], da)

    given = (da, n1, cosine, sine, aux, row, q, k, v, o, lse)
    given += (w_attn,) * 6
    so_far = []
    for first, count in SPLIT:
        closing = (part, x_low, gain_one, pick)
        grad_attn, dn1, *ends = attend_back(first, count, given, so_far, closing, blocks)
        if first + count < KV_HEADS:
            dn1 = wait([wide, down], dn1)
            dn1 = start_ahead([wide, down], dn1)
        so_far = [dn1, grad_attn]
    columns, one = ends
    grad_attn = wait([wide, down], grad_attn)
    attn = Scatter(*split_cores(grad_attn, bits), bits, late=True)
    scalars = scalars.at[0].add(jnp.sum(sums[1]))
    total = Total(jnp.stack([one[0], two[0], sums[0], scalars], axis=0), bits)

    start(attn, wide, down, total)
    wait([attn, total])
    grad_home = to_home(columns)
    take(wide, down)
    while attn.step < len(bits):
        start(attn, wide, down, total)
        if attn.step < len(bits):
            wait([attn, total])
            take(wide, down)
    grad_home, attn.mine = join(grad_home, attn.mine)
    take(attn, wide, down, total)
    finish(attn, wide, down, total)
    attn_part, gu_part, down_part = attn.part, wide.part, down.part

    states_out = jnp.where(still, states, out_home)
    states_grad = jnp.where(still, apart, grad_home.astype(F32))

    small = total.part
    mse_loss = 2.0 * small[3, 0] / (small[3, 1] * D)
    return (
        states_out,
        mse_loss,
        states_grad,
        attn_part.T,
        gu_part.T,
        down_part.T,
        small[0:2],
        small[2],
    )


def solution(mesh):
    tokens = P("dp", "ctx", None)
    flags = P("dp", "ctx")
    packs = P(None, ("dp", "ctx"))
    return jax.shard_map(
        on_device,
        mesh=mesh,
        in_specs=(tokens, tokens, flags, flags, packs, packs, packs, P(), P()),
        out_specs=(tokens, P(), tokens, packs, packs, packs, P(), P()),
        check_vma=False,
    )
```

```python
import functools

import jax
import jax.numpy as jnp
from jax import lax
from jax.experimental import pallas as pl
from jax.experimental.pallas import tpu as pltpu
from jax.sharding import PartitionSpec as P

D = 960
HEADS = 15
KV_HEADS = 5
HEAD = 64
FF = 2560
CHOSEN = 640
PER_KV = HEADS // KV_HEADS
KV_WIDTH = KV_HEADS * HEAD
QKV_COLS = D + 2 * KV_WIDTH
ROWS = 656
TILE = 256
WIDE = 768
SLAB = 1280
SPLIT = ((0, 3), (3, 2))
CHUNK = 640
TILES = ((0, 256, 512), (256, 512, 768), (512, ROWS, 768))
NEG = -1e30
VMEM_LIMIT = 62 * 1024 * 1024

EPS = 1e-05
THETA = 10000.0
F32 = jnp.float32
BF16 = jnp.bfloat16


def device_bits():
    found = []
    for name in ("dp", "ctx"):
        count = lax.axis_size(name)
        found += [(name, bit) for bit in reversed(range(count.bit_length() - 1))]
    return found


def swap(value, place):
    name, bit = place
    pairs = [(i, i ^ (1 << bit)) for i in range(lax.axis_size(name))]
    return lax.ppermute(value, name, pairs)


def own_bit(place):
    name, bit = place
    return (lax.axis_index(name) >> bit) & 1


def routes(bits):
    count = len(bits)
    far = list(range(1, count - 3))
    return [far + [count - 3, count - 2, count - 1], far + [count - 2, count - 3, count - 1]]


def late_routes(bits):
    count = len(bits)
    far = list(range(count - 4, 0, -1))
    return [[count - 3] + far + [count - 2], far + [count - 3, count - 2]]


def join(*values):
    return lax.optimization_barrier(values)


def own_bits(bits):
    return jnp.stack([own_bit(place) for place in bits]).astype(jnp.int32)


def order_kernel(spots, own, mine0, other0, mine1, other1, out, sems):
    last = len(spots[0])

    def copies(place):
        found = []
        for half, (mine, other) in enumerate(((mine0, other0), (mine1, other1))):
            slot = 0
            for level, spot in enumerate(spots[half]):
                slot = slot + ((((place >> level) & 1) ^ own[spot]) << (last - spot))
            core = own[last + 1]
            for k, (source, side) in enumerate(((mine, core), (other, 1 - core))):
                found.append(
                    pltpu.make_async_copy(
                        source.at[place], out.at[half, slot, side], sems.at[2 * half + k, place]
                    )
                )
        return found

    def begin(place, carry):
        for copy in copies(place):
            copy.start()
        return carry

    def end(place, carry):
        for copy in copies(place):
            copy.wait()
        return carry

    count = mine0.shape[0]
    lax.fori_loop(0, count, begin, 0)
    lax.fori_loop(0, count, end, 0)


class Gather:
    def __init__(self, shard, bits):
        self.bits = bits
        self.halves, self.routes = [shard[None]], routes(bits)
        self.step, self.part = 0, None
        self.got = []

    def send(self):
        if self.step == 0:
            self.got = [swap(self.halves[0], self.bits[0])]
        else:
            spots = [route[self.step - 1] for route in self.routes]
            self.got = [swap(h, self.bits[s]) for h, s in zip(self.halves, spots)]
        self.step += 1

    def take(self):
        if self.step == 1:
            low_side = own_bit(self.bits[0]) == 0
            shard, other = self.halves[0], self.got[0]
            self.halves = [jnp.where(low_side, shard, other), jnp.where(low_side, other, shard)]
        elif self.step < len(self.bits):
            self.halves = [jnp.concatenate(p, axis=0) for p in zip(self.halves, self.got)]
        else:
            self.part = self.ordered()

    def ordered(self):
        count, rows, width = self.halves[0].shape
        anywhere = pl.BlockSpec(memory_space=pl.ANY)
        out = pl.pallas_call(
            functools.partial(order_kernel, [r[:-1] for r in self.routes]),
            in_specs=[pl.BlockSpec(memory_space=pltpu.SMEM)] + [anywhere] * 4,
            out_specs=pl.BlockSpec(memory_space=pltpu.VMEM),
            out_shape=jax.ShapeDtypeStruct((2, count, 2, rows, width), BF16),
            scratch_shapes=[pltpu.SemaphoreType.DMA((4, count))],
            compiler_params=pltpu.CompilerParams(vmem_limit_bytes=VMEM_LIMIT),
            name="order",
        )(own_bits(self.bits), self.halves[0], self.got[0], self.halves[1], self.got[1])
        return out.reshape(-1, width)


class Scatter:
    def __init__(self, keep, send, bits, late=False):
        self.bits = bits
        self.keep, self.out = keep, send
        self.routes = late_routes(bits) if late else [route[-2::-1] for route in routes(bits)]
        self.step, self.part = 0, None
        self.got, self.outs = [], []

    def choose(self, half, choice):
        total = 0.0
        for array, held in self.parts[half]:
            rows, width = array.shape[-2:]
            run = [h for h in held if h in choice]
            if run:
                at, index = held.index(run[0]), 0
                for spot in run:
                    index = 2 * index + choice[spot]
                cube = array.reshape(1 << at, 1 << len(run), -1, width)
                array = lax.dynamic_index_in_dim(cube, index, 1, keepdims=False)
            total = total + array.reshape(-1, rows, width).astype(F32)
        return total

    def cut(self):
        last = len(self.bits) - 1
        if self.step == 0:
            self.outs, self.spots = [self.out], [last]
        elif self.step < last:
            self.outs, self.spots = [], []
            for half, route in enumerate(self.routes):
                choice = {s: own_bit(self.bits[s]) for s in route[: self.step]}
                spot = route[self.step - 1]
                choice[spot] = 1 - choice[spot]
                self.outs.append(self.choose(half, choice).astype(BF16))
                self.spots.append(spot)
        else:
            low_side = own_bit(self.bits[0]) == 0
            sums = []
            for half, route in enumerate(self.routes):
                sums.append(self.choose(half, {s: own_bit(self.bits[s]) for s in route})[0])
            self.mine = jnp.where(low_side, sums[0], sums[1])
            self.outs = [jnp.where(low_side, sums[1], sums[0]).astype(BF16)]
            self.spots = [0]

    def send(self):
        if not self.outs:
            self.cut()
        self.got = [swap(out, self.bits[spot]) for out, spot in zip(self.outs, self.spots)]
        self.outs = []
        self.step += 1

    def take(self):
        if self.step == 1:
            held = sorted(self.routes[0])
            self.parts = [
                [(self.keep[half], held), (self.got[0][half], held)] for half in range(2)
            ]
        elif self.step <= len(self.bits) - 1:
            for parts, got, route in zip(self.parts, self.got, self.routes):
                parts.append((got, sorted(route[self.step - 1 :])))
        else:
            self.part = self.mine + self.got[0].astype(F32)


def split_cores(whole, bits):
    count = 1 << (len(bits) - 2)
    cube = whole.reshape(2 * count, 2, -1, whole.shape[-1])
    mine = own_bit(bits[-1])
    both = [lax.dynamic_index_in_dim(cube, side, 1, keepdims=False) for side in (mine, 1 - mine)]
    return [b.reshape(2, count, -1, whole.shape[-1]) for b in both]


def start(*moves):
    for m in moves:
        if m.part is None and not m.got:
            m.send()


def start_ahead(moves, *values):
    moves = [m for m in moves if m.part is None and not m.got]
    for m in moves:
        m.cut()
    flat = list(join(*values, *[o for m in moves for o in m.outs]))
    values, flat = flat[: len(values)], flat[len(values) :]
    for m in moves:
        m.outs, flat = flat[: len(m.outs)], flat[len(m.outs) :]
        m.send()
    return values if len(values) != 1 else values[0]


def take(*moves):
    for m in moves:
        if m.got:
            m.take()
            m.got = []


def wait(moves, *values):
    moves = [m for m in moves if m.got]
    flat = list(join(*values, *[g for m in moves for g in m.got]))
    values, flat = flat[: len(values)], flat[len(values) :]
    for m in moves:
        m.got, flat = flat[: len(m.got)], flat[len(m.got) :]
    take(*moves)
    return values if len(values) != 1 else values[0]


def finish(*moves):
    while any(m.part is None for m in moves):
        start(*moves)
        take(*moves)


class Total:
    def __init__(self, value, bits):
        self.value, self.bits = value, bits
        self.step, self.part, self.got = 0, None, []

    def send(self):
        self.got = [swap(self.value, self.bits[self.step])]
        self.step += 1

    def take(self):
        self.value = self.value + self.got[0]
        if self.step == len(self.bits):
            self.part = self.value


def dot(left, right, contract):
    return lax.dot_general(left, right, (contract, ((), ())), preferred_element_type=F32)


def to_sequence(blocks):
    return lax.all_to_all(blocks, "ctx", split_axis=0, concat_axis=0, tiled=True)


def nt(left, right):
    return lax.dot_general(left, right, (((1,), (1,)), ((), ())), preferred_element_type=F32)


def nn(left, right):
    return lax.dot_general(left, right, (((1,), (0,)), ((), ())), preferred_element_type=F32)


def tn(left, right):
    return lax.dot_general(left, right, (((0,), (0,)), ((), ())), preferred_element_type=F32)


def turned(values, cosine, sine):
    half = HEAD // 2
    pieces = []
    for start in range(0, values.shape[1], HEAD):
        head = values[:, start : start + HEAD]
        swapped = jnp.concatenate([head[:, half:], head[:, :half]], axis=1)
        pieces.append(head * cosine + swapped * sine)
    return pieces


def weight_specs(first):
    places = [HEADS, HEADS + KV_HEADS] + [QKV_COLS // HEAD + r for r in range(PER_KV)]
    steps = [1, 1] + [PER_KV] * PER_KV
    return [pl.BlockSpec((D // KV_HEADS, D), lambda g: (first + g, 0))] + [
        pl.BlockSpec((HEAD, D), lambda g, p=p, s=s: (p + s * (first + g), 0))
        for p, s in zip(places, steps)
    ]


def attend_kernel(
    x_ref, gain_ref, cos_ref, sin_ref, aux_ref, row_ref, wq_ref, wk_ref, wv_ref, wo0_ref, wo1_ref, wo2_ref,
    n1_ref, q_ref, k_ref, v_ref, o_ref, l_ref, h1_ref,
    bias, keys, vals, lse,
):
    group = pl.program_id(0)

    @pl.when(group == 0)
    def _():
        x = x_ref[...].astype(F32)
        inv = lax.rsqrt(jnp.mean(x * x, axis=-1, keepdims=True) + EPS)
        n1_ref[...] = (x * inv * gain_ref[...]).astype(BF16)
        h1_ref[...] = x
        bias[...] = jnp.where(row_ref[1:2, :] <= aux_ref[:, 2:3], 0.0, NEG)
        keys[...] = jnp.zeros_like(keys)
        vals[...] = jnp.zeros_like(vals)
        lse[...] = jnp.zeros_like(lse)

    packed = jnp.concatenate([wq_ref[...], wk_ref[...], wv_ref[...]], axis=0)
    mixed = nt(n1_ref[...], packed)
    rotated = turned(mixed[:, : D // KV_HEADS + HEAD], cos_ref[...], sin_ref[...])
    key = rotated[PER_KV].astype(BF16)
    value = mixed[:, D // KV_HEADS + HEAD :].astype(BF16)
    k_ref[0] = key
    v_ref[0] = value
    keys[:ROWS] = key
    vals[:ROWS] = value
    for head in range(PER_KV):
        q_ref[head] = (rotated[head] * 0.125).astype(BF16)
    lanes = lax.broadcasted_iota(jnp.int32, (1, 128), 1)
    for start, stop, reach in TILES:
        outs = []
        logs = jnp.zeros((stop - start, 128), F32)
        for head in range(PER_KV):
            scores = nt(q_ref[head, start:stop], keys[:reach]) + bias[start:stop, :reach]
            top = jnp.max(scores, axis=-1, keepdims=True)
            expd = jnp.exp(scores - top)
            total = jnp.sum(expd, axis=-1, keepdims=True)
            outs.append(nn(expd.astype(BF16), vals[:reach]) / total)
            logs = jnp.where(lanes == head, top + jnp.log(total), logs)
        o_ref[0, start:stop] = jnp.concatenate(outs, axis=1).astype(BF16)
        lse[start:stop] = logs
    l_ref[0] = lse[...].T[:8]
    h1_ref[...] += nn(o_ref[0], jnp.concatenate([wo0_ref[...], wo1_ref[...], wo2_ref[...]], axis=0))


def attend(x, gain, cosine, sine, aux, row, w_attn):
    whole = lambda *shape: pl.BlockSpec(shape, lambda g: (0,) * len(shape))
    fixed = lambda *shape: pl.BlockSpec(
        shape, lambda g: (0,) * len(shape), pipeline_mode=pl.Buffered(1)
    )
    per = D // KV_HEADS
    return pl.pallas_call(
        attend_kernel,
        grid=(KV_HEADS,),
        in_specs=[
            fixed(ROWS, D),
            fixed(1, D),
            fixed(ROWS, HEAD),
            fixed(ROWS, HEAD),
            fixed(ROWS, 8),
            fixed(8, WIDE),
            *weight_specs(0),
        ],
        out_specs=[
            whole(ROWS, D),
            pl.BlockSpec((PER_KV, ROWS, HEAD), lambda g: (g, 0, 0)),
            pl.BlockSpec((1, ROWS, HEAD), lambda g: (g, 0, 0)),
            pl.BlockSpec((1, ROWS, HEAD), lambda g: (g, 0, 0)),
            pl.BlockSpec((1, ROWS, per), lambda g: (g, 0, 0)),
            pl.BlockSpec((1, 8, WIDE), lambda g: (g, 0, 0)),
            whole(ROWS, D),
        ],
        out_shape=[
            jax.ShapeDtypeStruct((ROWS, D), BF16),
            jax.ShapeDtypeStruct((HEADS, ROWS, HEAD), BF16),
            jax.ShapeDtypeStruct((KV_HEADS, ROWS, HEAD), BF16),
            jax.ShapeDtypeStruct((KV_HEADS, ROWS, HEAD), BF16),
            jax.ShapeDtypeStruct((KV_HEADS, ROWS, per), BF16),
            jax.ShapeDtypeStruct((KV_HEADS, 8, WIDE), F32),
            jax.ShapeDtypeStruct((ROWS, D), F32),
        ],
        scratch_shapes=[
            pltpu.VMEM((ROWS, WIDE), F32),
            pltpu.VMEM((WIDE, HEAD), BF16),
            pltpu.VMEM((WIDE, HEAD), BF16),
            pltpu.VMEM((WIDE, 128), F32),
        ],
        compiler_params=pltpu.CompilerParams(vmem_limit_bytes=VMEM_LIMIT),
        name="attend",
    )(x, gain, cosine, sine, aux, row, *[w_attn] * 6)


def feed_specs(packs):
    if packs[0].ndim == 2:
        return [
            pl.BlockSpec((SLAB, D), lambda j: (j, 0)),
            pl.BlockSpec((SLAB, D), lambda j: (FF // SLAB + j, 0)),
            pl.BlockSpec((SLAB, D), lambda j: (j, 0)),
        ]
    count, rows, _ = packs[0].shape
    thin = rows // 3
    return [
        pl.BlockSpec((SLAB // (2 * thin), 2 * thin, D), lambda j: (j, 0, 0)),
        pl.BlockSpec((SLAB // (2 * thin), 2 * thin, D), lambda j: (FF // SLAB + j, 0, 0)),
        pl.BlockSpec((SLAB // thin, thin, D), lambda j: (j, 2, 0)),
    ]


def rows_of(ref, start=0, size=SLAB):
    if len(ref.shape) == 2:
        return ref[start : start + size]
    each = ref.shape[1]
    return ref[start // each : (start + size) // each].reshape(size, D)


def spread(compact, pick_ref, out_ref):
    size = out_ref.shape[2]
    for block in range(out_ref.shape[0]):
        places = pick_ref[:, block * size : (block + 1) * size]
        out_ref[block] = tn(compact, places).astype(BF16)


def feed_kernel(
    h1_ref, x_ref, t_ref, aux_ref, gain_ref, router_ref, pick_ref, wg_ref, wu_ref, wd_ref,
    n2_ref, g_ref, u_ref, hid_ref, out_ref, diff_ref, cols_ref, sums_ref, d_ffn_ref,
):
    step = pl.program_id(0)

    @pl.when(step == 0)
    def _():
        h1 = h1_ref[...]
        inv = lax.rsqrt(jnp.mean(h1 * h1, axis=-1, keepdims=True) + EPS)
        n2_ref[...] = (h1 * inv * gain_ref[...]).astype(BF16)
        diff_ref[...] = h1 - x_ref[...].astype(F32)

    for start in range(0, SLAB, CHUNK):
        span = slice(start, start + CHUNK)
        gate = nt(n2_ref[...], rows_of(wg_ref, start, CHUNK))
        up = nt(n2_ref[...], rows_of(wu_ref, start, CHUNK))
        g_ref[:, span] = gate.astype(BF16)
        u_ref[:, span] = up.astype(BF16)
        hid_ref[:, span] = (gate * jax.nn.sigmoid(gate) * up).astype(BF16)
    diff_ref[...] += nn(hid_ref[...], rows_of(wd_ref))

    @pl.when(step == pl.num_programs(0) - 1)
    def _():
        x = x_ref[...].astype(F32)
        branch = diff_ref[...]
        valid, live = aux_ref[:, 0:1], aux_ref[:, 1:2]
        prob = jax.nn.sigmoid(jnp.sum(x * router_ref[...], axis=-1, keepdims=True))
        mix = live * prob
        result = x + mix * branch
        spread(result.astype(BF16), pick_ref, out_ref)
        diff = valid * (result - t_ref[...].astype(F32))
        d_logit = live * jnp.sum(diff * branch, axis=-1, keepdims=True) * prob * (1.0 - prob)
        diff_ref[...] = diff
        d_ffn_ref[...] = (mix * diff).astype(BF16)
        lanes = lax.broadcasted_iota(jnp.int32, (1, 128), 1)
        cols_ref[...] = jnp.where(lanes == 0, mix, jnp.where(lanes == 1, d_logit, 0.0))
        sums_ref[...] = jnp.concatenate(
            [
                jnp.sum(d_logit * x, axis=0, keepdims=True),
                0.5 * jnp.sum(diff * diff, axis=0, keepdims=True),
                jnp.zeros((6, D), F32),
            ],
            axis=0,
        )


def feed(h1, x, t, aux, gain, router, pick, packs, blocks):
    whole = lambda *shape: pl.BlockSpec(shape, lambda j: (0,) * len(shape))
    fixed = lambda *shape: pl.BlockSpec(
        shape, lambda j: (0,) * len(shape), pipeline_mode=pl.Buffered(1)
    )
    return pl.pallas_call(
        feed_kernel,
        grid=(FF // SLAB,),
        in_specs=[
            fixed(ROWS, D),
            fixed(ROWS, D),
            fixed(ROWS, D),
            fixed(ROWS, 8),
            fixed(1, D),
            fixed(1, D),
            fixed(*pick.shape),
            *feed_specs(packs),
        ],
        out_specs=[
            whole(ROWS, D),
            pl.BlockSpec((ROWS, SLAB), lambda j: (0, j)),
            pl.BlockSpec((ROWS, SLAB), lambda j: (0, j)),
            pl.BlockSpec((ROWS, SLAB), lambda j: (0, j)),
            whole(*blocks),
            whole(ROWS, D),
            whole(ROWS, 128),
            whole(8, D),
            whole(ROWS, D),
        ],
        out_shape=[
            jax.ShapeDtypeStruct((ROWS, D), BF16),
            jax.ShapeDtypeStruct((ROWS, FF), BF16),
            jax.ShapeDtypeStruct((ROWS, FF), BF16),
            jax.ShapeDtypeStruct((ROWS, FF), BF16),
            jax.ShapeDtypeStruct(blocks, BF16),
            jax.ShapeDtypeStruct((ROWS, D), F32),
            jax.ShapeDtypeStruct((ROWS, 128), F32),
            jax.ShapeDtypeStruct((8, D), F32),
            jax.ShapeDtypeStruct((ROWS, D), BF16),
        ],
        compiler_params=pltpu.CompilerParams(vmem_limit_bytes=VMEM_LIMIT),
        name="feed",
    )(h1, x, t, aux, gain, router, pick, *packs)


def shared_out(core_ref, total, refs, rows):
    low = core_ref[0] == 0
    for pair in range(total.shape[0] // (2 * rows)):
        even = total[2 * pair * rows : (2 * pair + 1) * rows]
        odd = total[(2 * pair + 1) * rows : (2 * pair + 2) * rows]
        refs[0][pair] = jnp.where(low, even, odd).astype(BF16)
        refs[1][pair] = jnp.where(low, odd, even).astype(BF16)


def down_grad_kernel(hid_ref, d_ffn_ref, core_ref, *outs):
    total = tn(hid_ref[...], d_ffn_ref[...])
    if len(outs) == 1:
        outs[0][...] = total.astype(BF16)
    else:
        shared_out(core_ref, total, outs, outs[0].shape[1])


def down_grad(hid, d_ffn, core, bits):
    rows = FF >> len(bits)
    shape, spec = (FF, D), pl.BlockSpec((CHUNK, D), lambda j: (j, 0))
    outs = 1
    if rows % 16 == 0:
        outs, shape = 2, (FF // (2 * rows), rows, D)
        spec = pl.BlockSpec((CHUNK // (2 * rows), rows, D), lambda j: (j, 0, 0))
    got = pl.pallas_call(
        down_grad_kernel,
        grid=(FF // CHUNK,),
        in_specs=[
            pl.BlockSpec((ROWS, CHUNK), lambda j: (0, j)),
            pl.BlockSpec((ROWS, D), lambda j: (0, 0)),
            pl.BlockSpec(memory_space=pltpu.SMEM),
        ],
        out_specs=[spec] * outs,
        out_shape=[jax.ShapeDtypeStruct(shape, BF16)] * outs,
        compiler_params=pltpu.CompilerParams(vmem_limit_bytes=VMEM_LIMIT),
        name="down_grad",
    )(hid, d_ffn, core)
    if outs == 1:
        return split_cores(got[0], bits)
    return [a.reshape(2, -1, rows, D) for a in got]


def feed_back_kernel(
    h1_ref, n2_ref, diff_ref, cols_ref, gain_ref, router_ref, g_ref, u_ref, d_ffn_ref,
    wg_ref, wu_ref, wd_ref, core_ref,
    *rest,
):
    *grads, da_ref, part_ref, sums_ref, d_gate, d_up = rest
    step = pl.program_id(0)

    @pl.when(step == 0)
    def _():
        part_ref[...] = jnp.zeros_like(part_ref)

    for start in range(0, SLAB, CHUNK):
        span = slice(start, start + CHUNK)
        d_hidden = nt(d_ffn_ref[...], rows_of(wd_ref, start, CHUNK))
        gate = g_ref[:, span].astype(F32)
        up = u_ref[:, span].astype(F32)
        sig = jax.nn.sigmoid(gate)
        d_gate[:, span] = (d_hidden * up * sig * (1.0 + gate * (1.0 - sig))).astype(BF16)
        d_up[:, span] = (d_hidden * gate * sig).astype(BF16)
        for half, source in enumerate((d_gate, d_up)):
            total = tn(source[:, span], n2_ref[...])
            if len(grads) == 1:
                grads[0][half, span] = total.astype(BF16)
            else:
                rows = grads[0].shape[2]
                spots = slice(start // (2 * rows), (start + CHUNK) // (2 * rows))
                shared_out(core_ref, total, [a.at[half, spots] for a in grads], rows)
    part_ref[...] += nn(d_gate[...], rows_of(wg_ref)) + nn(d_up[...], rows_of(wu_ref))

    @pl.when(step == pl.num_programs(0) - 1)
    def _():
        h1 = h1_ref[...]
        inv = lax.rsqrt(jnp.mean(h1 * h1, axis=-1, keepdims=True) + EPS)
        d_norm = part_ref[...]
        sums_ref[...] = jnp.broadcast_to(
            jnp.sum(d_norm * h1 * inv, axis=0, keepdims=True), sums_ref.shape
        )
        scaled = d_norm * gain_ref[...]
        d_inner = inv * scaled - h1 * inv**3 * jnp.mean(scaled * h1, axis=-1, keepdims=True)
        diff = diff_ref[...]
        da_ref[...] = (cols_ref[:, 0:1] * diff + d_inner).astype(BF16)
        part_ref[...] = diff + cols_ref[:, 1:2] * router_ref[...] + d_inner


def feed_back(h1, n2, diff, cols, gain, router, g, u, d_ffn, packs, core, bits):
    rows = 2 * FF >> len(bits)
    spec, outs, shape = pl.BlockSpec((2, SLAB, D), lambda j: (0, j, 0)), 1, (2, FF, D)
    if rows % 16 == 0:
        outs, shape = 2, (2, FF // (2 * rows), rows, D)
        spec = pl.BlockSpec((2, SLAB // (2 * rows), rows, D), lambda j: (0, j, 0, 0))
    whole = lambda *shape: pl.BlockSpec(shape, lambda j: (0,) * len(shape))
    fixed = lambda *shape: pl.BlockSpec(
        shape, lambda j: (0,) * len(shape), pipeline_mode=pl.Buffered(1)
    )
    *grads, da, part, sums = pl.pallas_call(
        feed_back_kernel,
        grid=(FF // SLAB,),
        in_specs=[
            fixed(ROWS, D),
            fixed(ROWS, D),
            fixed(ROWS, D),
            fixed(ROWS, 128),
            fixed(1, D),
            fixed(1, D),
            pl.BlockSpec((ROWS, SLAB), lambda j: (0, j)),
            pl.BlockSpec((ROWS, SLAB), lambda j: (0, j)),
            fixed(ROWS, D),
            *feed_specs(packs),
            pl.BlockSpec(memory_space=pltpu.SMEM),
        ],
        out_specs=[
            *[spec] * outs,
            whole(ROWS, D),
            whole(ROWS, D),
            whole(8, D),
        ],
        out_shape=[
            *[jax.ShapeDtypeStruct(shape, BF16)] * outs,
            jax.ShapeDtypeStruct((ROWS, D), BF16),
            jax.ShapeDtypeStruct((ROWS, D), F32),
            jax.ShapeDtypeStruct((8, D), F32),
        ],
        scratch_shapes=[
            pltpu.VMEM((ROWS, SLAB), BF16),
            pltpu.VMEM((ROWS, SLAB), BF16),
        ],
        compiler_params=pltpu.CompilerParams(vmem_limit_bytes=VMEM_LIMIT),
        name="feed_back",
    )(h1, n2, diff, cols, gain, router, g, u, d_ffn, *packs, core)
    if outs == 1:
        grads = split_cores(grads[0].reshape(2 * FF, D), bits)
    return [*grads, da, part, sums]


def attend_back_kernel(
    first, final, da_ref, n1_ref, cos_ref, sin_ref, aux_ref, row_ref,
    q_ref, k_ref, v_ref, o_ref, l_ref, wq_ref, wk_ref, wv_ref, wo0_ref, wo1_ref, wo2_ref,
    *rest,
):
    *rest, bias, wide_q, wide_do, dq, stage, sems = rest
    if final:
        *rest, part_ref, x_ref, gain_ref, pick_ref, pack_ref, dn1, grad_ref, sums_ref = rest
    else:
        *rest, pack_ref, dn1 = rest
    group = pl.program_id(0)
    per = D // KV_HEADS

    @pl.when(group == 0)
    def _():
        bias[...] = jnp.where(aux_ref[:, 3:4] <= row_ref[0:1, :], 0.0, NEG)
        wide_q[...] = jnp.zeros_like(wide_q)
        wide_do[...] = jnp.zeros_like(wide_do)
        dn1[...] = rest[0][...] if rest else jnp.zeros_like(dn1)

    w_out = jnp.concatenate([wo0_ref[...], wo1_ref[...], wo2_ref[...]], axis=0)
    d_heads = nt(da_ref[...], w_out)
    d_low = d_heads.astype(BF16)
    stage[per + 2 * HEAD :] = tn(o_ref[0], da_ref[...]).astype(BF16)
    copies, top = [], 0
    for rows, base in ((per, 0), (HEAD, D), (HEAD, D + KV_WIDTH), (per, QKV_COLS)):
        place = pl.multiple_of(base + (first + group) * rows, HEAD)
        copies.append(
            pltpu.make_async_copy(
                stage.at[top : top + rows], pack_ref.at[pl.ds(place, rows)], sems.at[len(copies)]
            )
        )
        top += rows
    copies[3].start()
    both = d_low.astype(F32) * o_ref[0].astype(F32)
    key, value = k_ref[0], v_ref[0]
    d_key = jnp.zeros((ROWS, HEAD), F32)
    d_value = jnp.zeros((ROWS, HEAD), F32)
    d_queries = []
    ones = jnp.ones((8, HEAD), F32)
    for head in range(PER_KV):
        span = slice(head * HEAD, (head + 1) * HEAD)
        wide_q[:ROWS] = q_ref[head]
        wide_do[:ROWS] = d_low[:, span]
        inside = lax.dot_general(
            ones, both[:, span], (((1,), (1,)), ((), ())),
            preferred_element_type=F32, precision=lax.Precision.HIGHEST,
        )
        inside = jnp.concatenate([inside, jnp.zeros((8, WIDE - ROWS), F32)], axis=1)
        for start, stop, reach in TILES:
            end = start + TILE
            reach = min(reach, ROWS)
            scores = nt(key[:reach], wide_q[start:end]) + bias[:reach, start:end]
            probs = jnp.exp(scores - l_ref[0, head : head + 1, start:end])
            d_probs = nt(value[:reach], wide_do[start:end])
            d_scores = (probs * (d_probs - inside[0:1, start:end])).astype(BF16)
            add_k = nn(d_scores, wide_q[start:end])
            add_v = nn(probs.astype(BF16), wide_do[start:end])
            if reach < ROWS:
                rest = jnp.zeros((ROWS - reach, HEAD), F32)
                add_k = jnp.concatenate([add_k, rest], axis=0)
                add_v = jnp.concatenate([add_v, rest], axis=0)
            d_key += add_k
            d_value += add_v
            dq[start:end] = tn(d_scores, key[:reach]) * 0.125
        d_queries.append(dq[:ROWS])
    turned_back = turned(
        jnp.concatenate(d_queries + [d_key], axis=1), cos_ref[...], -sin_ref[...]
    )
    d_mixed = jnp.concatenate(turned_back + [d_value], axis=1).astype(BF16)
    stage[: per + 2 * HEAD] = tn(d_mixed, n1_ref[...]).astype(BF16)
    for copy in copies[:3]:
        copy.start()
    packed = jnp.concatenate([wq_ref[...], wk_ref[...], wv_ref[...]], axis=0)
    dn1[...] += nn(d_mixed, packed)
    for copy in copies:
        copy.wait()

    if not final:
        return

    @pl.when(group == pl.num_programs(0) - 1)
    def _():
        x = x_ref[...].astype(F32)
        inv = lax.rsqrt(jnp.mean(x * x, axis=-1, keepdims=True) + EPS)
        d_norm = dn1[...]
        sums_ref[...] = jnp.broadcast_to(
            jnp.sum(d_norm * x * inv, axis=0, keepdims=True), sums_ref.shape
        )
        scaled = d_norm * gain_ref[...]
        d_x = inv * scaled - x * inv**3 * jnp.mean(scaled * x, axis=-1, keepdims=True)
        spread((part_ref[...] + d_x).astype(BF16), pick_ref, grad_ref)


def attend_back(first, count, given, so_far, closing, blocks):
    whole = lambda *shape: pl.BlockSpec(shape, lambda g: (0,) * len(shape))
    fixed = lambda *shape: pl.BlockSpec(
        shape, lambda g: (0,) * len(shape), pipeline_mode=pl.Buffered(1)
    )
    per = D // KV_HEADS
    final = first + count == KV_HEADS
    kept = pl.BlockSpec(memory_space=pl.ANY)
    return pl.pallas_call(
        functools.partial(attend_back_kernel, first, final),
        grid=(count,),
        in_specs=[
            fixed(ROWS, D),
            fixed(ROWS, D),
            fixed(ROWS, HEAD),
            fixed(ROWS, HEAD),
            fixed(ROWS, 8),
            fixed(8, WIDE),
            pl.BlockSpec((PER_KV, ROWS, HEAD), lambda g: (first + g, 0, 0)),
            pl.BlockSpec((1, ROWS, HEAD), lambda g: (first + g, 0, 0)),
            pl.BlockSpec((1, ROWS, HEAD), lambda g: (first + g, 0, 0)),
            pl.BlockSpec((1, ROWS, per), lambda g: (first + g, 0, 0)),
            pl.BlockSpec((1, 8, WIDE), lambda g: (first + g, 0, 0)),
            *weight_specs(first),
            *([fixed(ROWS, D), kept] if so_far else []),
            *([fixed(*c.shape) for c in closing] if final else []),
        ],
        out_specs=[
            kept,
            whole(ROWS, D),
            *([whole(*blocks), whole(8, D)] if final else []),
        ],
        out_shape=[
            jax.ShapeDtypeStruct((QKV_COLS + D, D), BF16),
            jax.ShapeDtypeStruct((ROWS, D), F32),
            *(
                [jax.ShapeDtypeStruct(blocks, BF16), jax.ShapeDtypeStruct((8, D), F32)]
                if final
                else []
            ),
        ],
        scratch_shapes=[
            pltpu.VMEM((ROWS, WIDE), F32),
            pltpu.VMEM((WIDE, HEAD), BF16),
            pltpu.VMEM((WIDE, HEAD), BF16),
            pltpu.VMEM((WIDE, HEAD), F32),
            pltpu.VMEM((2 * (per + HEAD), D), BF16),
            pltpu.SemaphoreType.DMA((4,)),
        ],
        input_output_aliases={18: 0} if so_far else {},
        compiler_params=pltpu.CompilerParams(vmem_limit_bytes=VMEM_LIMIT),
        name="attend_back",
    )(*given, *so_far, *(closing if final else ()))


def on_device(states, teacher, validity, chosen, attn_pack, gate_up, down_proj, norm_gains, router):
    seq_count, block_rows, width = states.shape
    ctx_count = lax.axis_size("ctx")
    if seq_count != ctx_count:
        raise ValueError("seq_count")
    seq_length = block_rows * ctx_count
    bits = device_bits()
    gain_one, gain_two = norm_gains[0:1], norm_gains[1:2]
    core = own_bit(bits[-1]).astype(jnp.int32).reshape(1)

    feed_rows = jnp.concatenate([gate_up.T, down_proj.T], axis=0)
    packs = lax.all_gather(feed_rows, ("dp", "ctx"), axis=0)
    thin = down_proj.shape[1]
    if thin % 16:
        broad = packs[:, : 2 * thin].reshape(2 * FF, width)
        packs = (broad, broad, packs[:, 2 * thin :].reshape(FF, width))
    else:
        packs = (packs,) * 3
    flags = to_sequence((validity + 2 * chosen).reshape(seq_count, 1, block_rows))
    x_seq = to_sequence(states).reshape(seq_length, width)
    attn_in = Gather(attn_pack.T, bits)
    start(attn_in)
    flags = wait([attn_in], flags)
    start(attn_in)
    wait([attn_in])
    start(attn_in)

    flags = flags.reshape(seq_length)
    chosen_seq, valid_seq = flags >> 1, flags & 1
    place = jnp.arange(seq_length)
    rank = jnp.sum(jnp.where(place[:, None] < place[None, :], chosen_seq[:, None], 0), axis=0)
    slot = jnp.where(chosen_seq > 0, rank, -1)
    pick = (jnp.arange(ROWS)[:, None] == slot[None, :]).astype(BF16)
    picked = pick.astype(F32)
    pos = jnp.sum(picked * place.astype(F32)[None, :], axis=1)
    valid = jnp.sum(picked * valid_seq.astype(F32)[None, :], axis=1)
    live = (jnp.arange(ROWS) < jnp.sum(chosen_seq)).astype(F32)
    half = HEAD // 2
    freqs = THETA ** (-(jnp.arange(half).astype(F32) * 2.0 / HEAD))
    angles = pos[:, None] * freqs[None, :]
    cosine, sine = jnp.cos(angles), jnp.sin(angles)
    cosine = jnp.concatenate([cosine, cosine], axis=1)
    sine = jnp.concatenate([-sine, sine], axis=1)
    block = jnp.floor(pos / block_rows)
    key_block = jnp.where(valid * live > 0.5, block, 1e6)
    aux = jnp.stack([valid, live, block, key_block] + [jnp.zeros_like(pos)] * 4, axis=1)
    row = jnp.stack([block, key_block] + [jnp.zeros_like(pos)] * 6, axis=0)
    row = jnp.pad(row, ((0, 0), (0, WIDE - ROWS)), constant_values=1e6)
    router_row = router[None, :]


    x_home = states.astype(F32)
    still = (chosen == 0)[..., None]
    valid_home = validity.astype(F32)[..., None]
    apart = valid_home * (x_home - teacher.astype(F32))
    energy = 0.5 * jnp.sum(jnp.where(still, apart * apart, 0.0))
    scalars = jnp.concatenate(
        [energy[None], jnp.sum(validity).astype(F32)[None], jnp.zeros((D - 2,), F32)]
    )

    x_seq, pick, cosine, sine, aux, row, scalars = wait(
        [attn_in], x_seq, pick, cosine, sine, aux, row, scalars
    )
    start(attn_in)
    x_low = dot(pick, x_seq, ((1,), (0,))).astype(BF16)
    x_low = wait([attn_in], x_low)
    start(attn_in)
    wait([attn_in])
    finish(attn_in)
    w_attn = attn_in.part
    (late,) = join(teacher, w_attn)[:1]
    t_seq = to_sequence(late).reshape(seq_length, width)

    n1, q, k, v, o, lse, h1 = attend(x_low, gain_one, cosine, sine, aux, row, w_attn)
    t_low = dot(pick, t_seq, ((1,), (0,))).astype(BF16)
    blocks = (ctx_count, width, block_rows)
    n2, g, u, hid, out_columns, diff, cols, sums, d_ffn = feed(
        h1, x_low, t_low, aux, gain_two, router_row, pick, packs, blocks
    )

    def to_home(columns):
        return to_sequence(columns.transpose(0, 2, 1))

    down = Scatter(*down_grad(hid, d_ffn, core, bits), bits)
    start(down)
    d_ffn = wait([down], d_ffn)
    out_home = to_home(out_columns)
    d_ffn = start_ahead([down], d_ffn)
    *grad_gu, da, part, two = feed_back(
        h1, n2, diff, cols, gain_two, router_row, g, u, d_ffn, packs, core, bits
    )
    da, out_home, *grad_gu = wait([down], da, out_home, *grad_gu)
    wide = Scatter(*grad_gu, bits)
    start(wide, down)
    da = wait([wide], da)
    da = start_ahead([wide], da)

    given = (da, n1, cosine, sine, aux, row, q, k, v, o, lse)
    given += (w_attn,) * 6
    so_far = []
    for first, count in SPLIT:
        closing = (part, x_low, gain_one, pick)
        grad_attn, dn1, *ends = attend_back(first, count, given, so_far, closing, blocks)
        if first + count < KV_HEADS:
            dn1 = wait([wide, down], dn1)
            dn1 = start_ahead([wide, down], dn1)
        so_far = [dn1, grad_attn]
    columns, one = ends
    grad_attn = wait([wide, down], grad_attn)
    attn = Scatter(*split_cores(grad_attn, bits), bits, late=True)
    scalars = scalars.at[0].add(jnp.sum(sums[1]))
    total = Total(jnp.stack([one[0], two[0], sums[0], scalars], axis=0), bits)

    start(attn, wide, down, total)
    wait([attn, total])
    grad_home = to_home(columns)
    take(wide, down)
    while attn.step < len(bits):
        start(attn, wide, down, total)
        if attn.step < len(bits):
            out_home = wait([attn, total], out_home)
            take(wide, down)
    grad_home, attn.mine = join(grad_home, attn.mine)
    take(attn, wide, down, total)
    finish(attn, wide, down, total)
    attn_part, gu_part, down_part = attn.part, wide.part, down.part

    states_out = jnp.where(still, states, out_home)
    states_grad = jnp.where(still, apart, grad_home.astype(F32))

    small = total.part
    mse_loss = 2.0 * small[3, 0] / (small[3, 1] * D)
    return (
        states_out,
        mse_loss,
        states_grad,
        attn_part.T,
        gu_part.T,
        down_part.T,
        small[0:2],
        small[2],
    )


def solution(mesh):
    tokens = P("dp", "ctx", None)
    flags = P("dp", "ctx")
    packs = P(None, ("dp", "ctx"))
    return jax.shard_map(
        on_device,
        mesh=mesh,
        in_specs=(tokens, tokens, flags, flags, packs, packs, packs, P(), P()),
        out_specs=(tokens, P(), tokens, packs, packs, packs, P(), P()),
        check_vma=False,
    )
```
